512 devices in a mesh: dp: 16 (over y, core), expert: 32 (over x, z).
Axes of the slice: x: 4, y: 8, z: 8, core: 2. Of those that a mesh axis runs over, the one named last changes fastest.
Arguments:
- tokens: bfloat16 [32768, 2048], P(('dp', 'expert')), may hold values from -6 to 6
- expert_ids: int32 [32768, 8], P(('dp', 'expert')), may hold values from 0 to 127, all different within a row; in each aligned block of 64 rows (0 to 63, 64 to 127, ...) at most 8 rows name the same one
- gate_weight: bfloat16 [32, 2048, 768], P('expert', 'dp'), may hold values from -0.125 to 0.125
- up_weight: bfloat16 [32, 2048, 768], P('expert', 'dp'), may hold values from -0.125 to 0.125
- down_weight: bfloat16 [32, 768, 2048], P('expert', None, 'dp'), may hold values from -6 to 6
Outputs:
- factor: float32 [32, 768, 768], P('expert', 'dp')
- whitened: float32 [32, 768, 2048], P('expert', None, 'dp')
The draws below stay inside these ranges and needn't reach their ends.
Inputs may be any that keep to these rules, and one draw needn't show every extreme that they name: `expert_ids`: each row names 8 different experts. Among the rows of one device (aligned blocks of 64 rows) no expert is named more than 8 times, a bound that some block reaches. Only experts below 32 enter the outputs.
All inputs are finite; a program needn't handle non-finite values.
Results may differ from the reference program's by a relative error of at most 0.0035.
Values may be sent and summed in bfloat16 or wider, within the bound.
A program may use at most 128 MiB of HBM per device.

```python
import math
import jax
import jax.numpy as jnp
import numpy as np
from jax import lax

D = 2048
FW = 768
EXPERTS_ALL = 128
TOP = 8
TOK_DEV = 64
CAP = 8
EXPERTS = 32
TOKENS = 32768
SLOTS_DEV = 256
N_DP = 16
N_EXPERT = 32


def levels(key, shape, shards, low, top_value):
    level, own = 1.0, jax.random.fold_in(key, 6)
    for axis_at, blocks in shards:
        heights = jnp.exp(jax.random.uniform(jax.random.fold_in(own, axis_at), (blocks,), jnp.float32, low / len(shards), top_value / len(shards)))
        level = level * jnp.repeat(heights, shape[axis_at] // blocks).reshape([-1 if axis == axis_at else 1 for axis in range(len(shape))])
    return level


def shared_out(own_key, own, number, rows, amount, top, limit, skew):
    ranking = jax.random.permutation(own_key, amount)
    packed, usual = load_shares(amount, rows * top, limit, skew, True), load_shares(amount, rows * top, limit, skew, False)
    places = jnp.arange(amount)

    def named(sizes, rotation):
        used = int((sizes > 0).sum())
        fixed = max(1, used // 4)
        shifted = fixed + (places - fixed + rotation * (used - fixed)) % max(1, amount - fixed)
        return jnp.zeros((amount,), jnp.int32).at[ranking[jnp.where(places < fixed, places, shifted)]].set(jnp.asarray(sizes, jnp.int32))

    sizes = jnp.where(number % 4 == 0, named(packed, number // 4), named(usual, number - number // 4 - 1))
    mixed = jax.random.permutation(jax.random.fold_in(own, 3), amount)
    source_of, receiver = mixed[0:amount // 2 * 2:2], mixed[1:amount // 2 * 2:2]
    room = jnp.minimum(sizes[source_of] - 1, limit - sizes[receiver]) // 2
    room = jnp.where((source_of == ranking[0]) | (receiver == ranking[0]) | (sizes[receiver] == 0), 0, jnp.maximum(room, 0))
    shifted = jax.random.randint(jax.random.fold_in(own, 4), (amount // 2,), 0, 1 << 20) % (room + 1)
    sizes = sizes.at[source_of].add(-shifted).at[receiver].add(shifted)
    members = jnp.searchsorted(jnp.cumsum(sizes), jnp.arange(rows * top), side="right").astype(jnp.int32)
    listing = members.reshape(top, rows).T
    listing = listing[jax.random.permutation(jax.random.fold_in(own, 1), rows)]
    rotation = jax.random.randint(jax.random.fold_in(own, 2), (rows, 1), 0, top)
    return jnp.take_along_axis(listing, (jnp.arange(top)[None, :] + rotation) % top, axis=1)


def load_shares(count, total, reach, skew, full):
    weights = [(1 << 20) // math.isqrt(standing ** skew) + 1 for standing in range(1, count + 1)]
    largest = reach if full else min(reach, max(-(-total // count), total * weights[0] // sum(weights)))
    least = 1 if total - largest >= count - 1 else 0
    given, surplus = [largest] + [least] * (count - 1), total - largest - least * (count - 1)
    while surplus > 0:
        candidates = [i for i in range(1, count) if given[i] < largest] or [i for i in range(1, count) if given[i] < reach]
        pool, budget = sum([weights[i] for i in candidates]), surplus
        for i in candidates:
            more = min(reach - given[i], max(1, budget * weights[i] // pool), surplus)
            given[i] = given[i] + more
            surplus = surplus - more
    return np.array(given)


def scatter_about(stream_key, dims, scale, limit, pieces=(), kind=jnp.bfloat16):
    level = levels(stream_key, dims, pieces, -0.22, 0.18) if pieces else 1.0
    values = jax.random.normal(stream_key, dims, jnp.float32) * scale * level
    return jnp.minimum(jnp.maximum(values, -limit), limit).astype(kind)


def setup_inputs(seed: int = 0) -> dict:
    key_list = jax.random.split(jax.random.key(seed), 6)
    tokens = scatter_about(key_list[0], (TOKENS, D), 1.0, 6.0, ((0, 512),))
    expert_ids_keys = jax.random.split(jax.random.fold_in(key_list[1], 1), TOKENS // TOK_DEV)
    expert_ids_turns = jax.random.permutation(jax.random.fold_in(key_list[1], 3), TOKENS // TOK_DEV)
    expert_ids = jax.vmap(lambda own, number: shared_out(jax.random.fold_in(key_list[1], 2), own, number, TOK_DEV, EXPERTS_ALL, TOP, CAP, 2))(expert_ids_keys, expert_ids_turns).reshape((TOKENS, TOP))
    gate_weight = scatter_about(key_list[2], (EXPERTS, D, FW), D ** -0.5, 0.125, ((0, 32), (1, 16)))
    up_weight = scatter_about(key_list[3], (EXPERTS, D, FW), D ** -0.5, 0.125, ((0, 32), (1, 16)))
    down_weight = scatter_about(key_list[4], (EXPERTS, FW, D), 1.0, 6.0, ((0, 32), (2, 16)))
    return dict(tokens=tokens, expert_ids=expert_ids, gate_weight=gate_weight, up_weight=up_weight, down_weight=down_weight)


damping = 0.02

def reference(tokens, expert_ids, gate_weight, up_weight, down_weight):
    slot_count = N_DP * N_EXPERT * CAP
    identity = jnp.eye(FW, dtype=jnp.float32)

    def per_expert(expert):
        member = jnp.any(expert_ids == expert, axis=1)
        chosen = jnp.nonzero(member, size=slot_count, fill_value=0)[0]
        is_valid = jnp.arange(slot_count) < jnp.sum(member.astype(jnp.int32))
        picked = tokens[chosen]
        gate_sum = jnp.dot(picked.astype(jnp.float32), gate_weight[expert].astype(jnp.float32), preferred_element_type=jnp.float32)
        up_sum = jnp.dot(picked.astype(jnp.float32), up_weight[expert].astype(jnp.float32), preferred_element_type=jnp.float32)
        hidden = (jax.nn.silu(gate_sum) * up_sum).astype(jnp.bfloat16)
        hidden = jnp.where(is_valid[:, None], hidden, jnp.zeros_like(hidden))
        hidden_f = hidden.astype(jnp.float32)
        gram_sum = jnp.einsum('rf,rg->fg', hidden_f, hidden_f) / SLOTS_DEV + damping * identity
        factor = jnp.linalg.cholesky(gram_sum).T
        whitened = jnp.dot(factor, down_weight[expert].astype(jnp.float32), precision=lax.Precision.HIGHEST)
        return (factor, whitened)
    factors, whitened = lax.map(per_expert, jnp.arange(EXPERTS, dtype=jnp.int32))
    return (factors, whitened)
```

```python
import jax
import jax.numpy as jnp
from jax import lax
from jax.experimental import pallas as pl
from jax.experimental.pallas import tpu as pltpu
from jax.sharding import PartitionSpec as P

F32, BF16 = jnp.float32, jnp.bfloat16
N, B, H = 768, 128, 64


def split(x):
    high = x.astype(BF16)
    return high, (x - high.astype(F32)).astype(BF16)


def dot3(left, right, dims):
    lh, ll = split(left)
    rh, rl = split(right)
    dot = lambda a, b: lax.dot_general(a, b, (dims, ((), ())), preferred_element_type=F32)
    return dot(lh, rh) + (dot(lh, rl) + dot(ll, rh))


NN, TN = ((1,), (0,)), ((0,), (0,))


def eliminate(rows8, first):
    tiles = list(rows8)
    sublane = lax.broadcasted_iota(jnp.int32, (8, 128), 0)
    lane_copy = lambda x, c: jnp.broadcast_to(x[:, c:c + 1], (8, 128))
    row_copy = lambda x, i: jnp.broadcast_to(x[i:i + 1, :], (8, 128))
    for s in range(8):
        base = first + 8 * s
        columns = [lane_copy(tiles[s], base + j) for j in range(8)]
        a = {(i, j): row_copy(columns[j], i) for j in range(8) for i in range(j, 8)}
        row = [row_copy(tiles[s], j) for j in range(8)]
        inv, low = [], {}
        for j in range(8):
            r = lax.rsqrt(a[j, j])
            inv.append(r)
            for i in range(j + 1, 8):
                low[i, j] = a[i, j] * r
            for jj in range(j + 1, 8):
                for i in range(jj, 8):
                    a[i, jj] = a[i, jj] - low[i, j] * low[jj, j]
            row[j] = row[j] * r
            for i in range(j + 1, 8):
                row[i] = row[i] - low[i, j] * row[j]
        for t in range(s + 1, 8):
            column = [lane_copy(tiles[t], base + j) for j in range(8)]
            total = tiles[t]
            for j in range(8):
                column[j] = column[j] * inv[j]
                for jj in range(j + 1, 8):
                    column[jj] = column[jj] - column[j] * low[jj, j]
                total = total - column[j] * row[j]
            tiles[t] = total
        done = row[0]
        for j in range(1, 8):
            done = jnp.where(sublane == j, row[j], done)
        tiles[s] = done
    return jnp.concatenate(tiles, axis=0)


def factor_block(block):
    lane = lax.broadcasted_iota(jnp.int32, (H, B), 1)
    row = lax.broadcasted_iota(jnp.int32, (H, B), 0)
    zero = jnp.zeros((H, B), F32)
    top, bottom = block[:H], block[H:]
    work = jnp.where(lane < H, top, jnp.where(lane == row + H, 1.0, 0.0))
    done0 = eliminate([work[8 * t:8 * t + 8] for t in range(8)], 0)
    inv0 = jnp.where(lane < H, 0.0, done0)
    upper0 = dot3(inv0, jnp.concatenate([zero, top], axis=0), NN)
    upper0 = jnp.where(lane < H, jnp.where(lane >= row, done0, 0.0), upper0)
    bottom = bottom - dot3(upper0, upper0, TN)[H:]
    mixed = dot3(upper0, inv0, TN)[H:]
    work = jnp.where(lane >= H, bottom, jnp.where(lane == row, 1.0, 0.0))
    done1 = eliminate([work[8 * t:8 * t + 8] for t in range(8)], H)
    upper1 = jnp.where(lane >= row + H, done1, 0.0)
    inv1 = jnp.where(lane < H, done1, 0.0)
    inv1 = inv1 - dot3(inv1, jnp.concatenate([mixed, zero], axis=0), NN)
    return jnp.concatenate([upper0, upper1], axis=0), jnp.concatenate([inv0, inv1], axis=0)


def factor_all(work_ref):
    count = N // B

    def step(q, carry):
        here = pl.ds(pl.multiple_of(q * B, B), B)
        upper, inverse = factor_block(work_ref[here, here])
        work_ref[here, here] = upper
        for static in range(count - 1):
            @pl.when(q == static)
            def _(static=static):
                own, after = slice(static * B, static * B + B), slice(static * B + B, N)
                strip = work_ref[own, after]
                strip = jnp.concatenate([strip[H:], strip[:H]], axis=0)
                strip = dot3(inverse, strip, NN)
                work_ref[own, after] = strip
                high, low = split(strip)
                dot = lambda a, b: lax.dot_general(a, b, (TN, ((), ())), preferred_element_type=F32)
                for i in range(static + 1, count):
                    at = (i - static - 1) * B
                    lh, ll, rh, rl = high[:, at:at + B], low[:, at:at + B], high[:, at:], low[:, at:]
                    work_ref[i * B:i * B + B, i * B:] -= dot(lh, rh) + (dot(lh, rl) + dot(ll, rh))
        return carry

    lax.fori_loop(0, count, step, 0)


def whiten(work_ref, down_ref, white_ref):
    for q in range(N // B):
        own = slice(q * B, q * B + B)
        high, low = split(work_ref[own, q * B:])
        down = down_ref[q * B:, :]
        white_ref[own, :] = jnp.dot(high, down, preferred_element_type=F32) + jnp.dot(low, down, preferred_element_type=F32)


def local_kernel(place_ref, gram_ref, down_ref, rows_ref, white_ref, work_ref):
    for i in range(N // B):
        work_ref[i * B:i * B + B, i * B:] = gram_ref[i * B:i * B + B, i * B:]
        if i:
            work_ref[i * B:i * B + B, :i * B] = jnp.zeros((B, i * B), F32)
    factor_all(work_ref)
    share = rows_ref.shape[0]
    rows_ref[...] = work_ref[pl.ds(pl.multiple_of(place_ref[0] * share, 8), share), :]
    whiten(work_ref, down_ref, white_ref)


def local_call(place, gram, down, share=48):
    vmem = pl.BlockSpec(memory_space=pltpu.VMEM)
    return pl.pallas_call(
        local_kernel,
        out_shape=(jax.ShapeDtypeStruct((share, N), F32), jax.ShapeDtypeStruct((N, down.shape[1]), F32)),
        in_specs=[pl.BlockSpec(memory_space=pltpu.SMEM), vmem, vmem],
        out_specs=(vmem, vmem),
        scratch_shapes=[pltpu.VMEM((N, N), F32)],
        compiler_params=pltpu.CompilerParams(vmem_limit_bytes=48 << 20),
    )(place, gram, down)


CAP = 8
damping = 0.02


def body(tokens, expert_ids, gate_weight, up_weight, down_weight):
    owners = lax.axis_size("expert") * gate_weight.shape[0]
    tok_rows = tokens.shape[0]
    capacity = CAP
    expert_range = jnp.arange(owners, dtype=jnp.int32)
    member = jnp.any(expert_ids[:, :, None] == expert_range[None, None, :], axis=1)
    earlier = (jnp.arange(tok_rows)[:, None] > jnp.arange(tok_rows)[None, :]).astype(jnp.int32)
    ranking = jnp.dot(earlier, member.astype(jnp.int32))
    slot_range = jnp.arange(capacity, dtype=jnp.int32)
    placing = (member[:, :, None] & (ranking[:, :, None] == slot_range[None, None, :])).astype(
        jnp.bfloat16
    )
    outgoing = jnp.einsum(
        "tec,td->ecd", placing, tokens, preferred_element_type=jnp.float32
    ).astype(jnp.bfloat16)
    arrived = lax.all_to_all(outgoing, "expert", split_axis=0, concat_axis=0, tiled=True)
    received_rows = arrived.reshape(-1, arrived.shape[-1])
    slot_total = received_rows.shape[0]
    gate_sum = jnp.dot(
        received_rows,
        lax.all_gather(gate_weight, "dp", axis=1, tiled=True)[0],
        preferred_element_type=jnp.float32,
    )
    up_sum = jnp.dot(
        received_rows,
        lax.all_gather(up_weight, "dp", axis=1, tiled=True)[0],
        preferred_element_type=jnp.float32,
    )
    gate_sum, up_sum = (gate_sum, up_sum)
    hidden = (jax.nn.silu(gate_sum) * up_sum).astype(jnp.bfloat16)
    hidden_width = hidden.shape[1]
    identity = jnp.eye(hidden_width, dtype=jnp.float32)
    local_gram = (
        jnp.einsum("rf,rg->fg", hidden, hidden, preferred_element_type=jnp.float32) / slot_total
    )
    running_gram = lax.psum(local_gram, "dp") + damping * identity
    place = lax.axis_index("dp").astype(jnp.int32).reshape(1)
    own_rows, whitened = local_call(place, running_gram, down_weight[0], hidden_width // lax.axis_size("dp"))
    return (own_rows[None], whitened[None])


def solution(mesh):
    return jax.shard_map(
        body,
        mesh=mesh,
        in_specs=(
            P(("dp", "expert"), None),
            P(("dp", "expert"), None),
            P("expert", "dp", None),
            P("expert", "dp", None),
            P("expert", None, "dp"),
        ),
        out_specs=(P("expert", "dp", None), P("expert", None, "dp")),
        check_vma=False,
    )
```

```python
import jax
import jax.numpy as jnp
from jax import lax
from jax.experimental import pallas as pl
from jax.experimental.pallas import tpu as pltpu
from jax.sharding import PartitionSpec as P

F32, BF16 = jnp.float32, jnp.bfloat16
N, B, H = 768, 128, 64
CAP = 8
SLOTS = 256
damping = 0.02


def split(x):
    high = x.astype(BF16)
    return high, (x - high.astype(F32)).astype(BF16)


def dot3(left, right, dims):
    lh, ll = split(left)
    rh, rl = split(right)
    dot = lambda a, b: lax.dot_general(a, b, (dims, ((), ())), preferred_element_type=F32)
    return dot(lh, rh) + (dot(lh, rl) + dot(ll, rh))


NN, TN = ((1,), (0,)), ((0,), (0,))


def eliminate(rows8, first):
    tiles = list(rows8)
    sublane = lax.broadcasted_iota(jnp.int32, (8, 128), 0)
    lane_copy = lambda x, c: jnp.broadcast_to(x[:, c:c + 1], (8, 128))
    row_copy = lambda x, i: jnp.broadcast_to(x[i:i + 1, :], (8, 128))
    for s in range(8):
        base = first + 8 * s
        columns = [lane_copy(tiles[s], base + j) for j in range(8)]
        a = {(i, j): row_copy(columns[j], i) for j in range(8) for i in range(j, 8)}
        row = [row_copy(tiles[s], j) for j in range(8)]
        inv, low = [], {}
        for j in range(8):
            r = lax.rsqrt(a[j, j])
            inv.append(r)
            for i in range(j + 1, 8):
                low[i, j] = a[i, j] * r
            for jj in range(j + 1, 8):
                for i in range(jj, 8):
                    a[i, jj] = a[i, jj] - low[i, j] * low[jj, j]
            row[j] = row[j] * r
            for i in range(j + 1, 8):
                row[i] = row[i] - low[i, j] * row[j]
        for t in range(s + 1, 8):
            column = [lane_copy(tiles[t], base + j) for j in range(8)]
            total = tiles[t]
            for j in range(8):
                column[j] = column[j] * inv[j]
                for jj in range(j + 1, 8):
                    column[jj] = column[jj] - column[j] * low[jj, j]
                total = total - column[j] * row[j]
            tiles[t] = total
        done = row[0]
        for j in range(1, 8):
            done = jnp.where(sublane == j, row[j], done)
        tiles[s] = done
    return jnp.concatenate(tiles, axis=0)


def factor_block(block):
    lane = lax.broadcasted_iota(jnp.int32, (H, B), 1)
    row = lax.broadcasted_iota(jnp.int32, (H, B), 0)
    zero = jnp.zeros((H, B), F32)
    top, bottom = block[:H], block[H:]
    work = jnp.where(lane < H, top, jnp.where(lane == row + H, 1.0, 0.0))
    done0 = eliminate([work[8 * t:8 * t + 8] for t in range(8)], 0)
    inv0 = jnp.where(lane < H, 0.0, done0)
    upper0 = dot3(inv0, jnp.concatenate([zero, top], axis=0), NN)
    upper0 = jnp.where(lane < H, jnp.where(lane >= row, done0, 0.0), upper0)
    bottom = bottom - dot3(upper0, upper0, TN)[H:]
    mixed = dot3(upper0, inv0, TN)[H:]
    work = jnp.where(lane >= H, bottom, jnp.where(lane == row, 1.0, 0.0))
    done1 = eliminate([work[8 * t:8 * t + 8] for t in range(8)], H)
    upper1 = jnp.where(lane >= row + H, done1, 0.0)
    inv1 = jnp.where(lane < H, done1, 0.0)
    inv1 = inv1 - dot3(inv1, jnp.concatenate([mixed, zero], axis=0), NN)
    return jnp.concatenate([upper0, upper1], axis=0), jnp.concatenate([inv0, inv1], axis=0)


def factor_all(work_ref):
    count = N // B

    def step(q, carry):
        here = pl.ds(pl.multiple_of(q * B, B), B)
        upper, inverse = factor_block(work_ref[here, here])
        work_ref[here, here] = upper
        for static in range(count - 1):
            @pl.when(q == static)
            def _(static=static):
                own, after = slice(static * B, static * B + B), slice(static * B + B, N)
                strip = work_ref[own, after]
                strip = jnp.concatenate([strip[H:], strip[:H]], axis=0)
                strip = dot3(inverse, strip, NN)
                work_ref[own, after] = strip
                high, low = split(strip)
                dot = lambda a, b: lax.dot_general(a, b, (TN, ((), ())), preferred_element_type=F32)
                for i in range(static + 1, count):
                    at = (i - static - 1) * B
                    lh, ll, rh, rl = high[:, at:at + B], low[:, at:at + B], high[:, at:], low[:, at:]
                    work_ref[i * B:i * B + B, i * B:] -= dot(lh, rh) + (dot(lh, rl) + dot(ll, rh))
        return carry

    lax.fori_loop(0, count, step, 0)


def whiten(work_ref, down_ref, white_ref):
    for q in range(N // B):
        own = slice(q * B, q * B + B)
        high, low = split(work_ref[own, q * B:])
        down = down_ref[q * B:, :]
        white_ref[own, :] = jnp.dot(high, down, preferred_element_type=F32) + jnp.dot(low, down, preferred_element_type=F32)


def local_kernel(place_ref, gram_ref, down_ref, rows_ref, white_ref, work_ref):
    diagonal = lax.broadcasted_iota(jnp.int32, (B, B), 0) == lax.broadcasted_iota(jnp.int32, (B, B), 1)
    for i in range(N // B):
        for j in range(i, N // B):
            block = gram_ref[:, block_at(i, j)].reshape(B, B) * (1.0 / SLOTS)
            if i == j:
                block = block + jnp.where(diagonal, damping, 0.0)
            work_ref[i * B:i * B + B, j * B:j * B + B] = block
        if i:
            work_ref[i * B:i * B + B, :i * B] = jnp.zeros((B, i * B), F32)
    factor_all(work_ref)
    share = rows_ref.shape[0]
    rows_ref[...] = work_ref[pl.ds(pl.multiple_of(place_ref[0] * share, 8), share), :]
    whiten(work_ref, down_ref, white_ref)


def local_call(place, gram, down, share=48):
    vmem = pl.BlockSpec(memory_space=pltpu.VMEM)
    return pl.pallas_call(
        local_kernel,
        out_shape=(jax.ShapeDtypeStruct((share, N), F32), jax.ShapeDtypeStruct((N, down.shape[1]), F32)),
        in_specs=[pl.BlockSpec(memory_space=pltpu.SMEM), vmem, vmem],
        out_specs=(vmem, vmem),
        scratch_shapes=[pltpu.VMEM((N, N), F32)],
        compiler_params=pltpu.CompilerParams(vmem_limit_bytes=48 << 20),
    )(place, gram, down)


MESH = pl.DeviceIdType.MESH


def block_at(i, j):
    return i * (N // B) - i * (i - 1) // 2 + j - i


def exchange_kernel(
    outgoing_ref, gate_ref, up_ref, gram_ref, tok, rows, weights, sums, hid, strips, parts,
    own_sem, swap_send, swap_recv, tok_send, tok_recv, pass_send, pass_recv, ring_send, ring_recv,
    hid_send, hid_recv, part_send, part_recv, share_send, share_recv,
):
    dp, e = lax.axis_index("dp"), lax.axis_index("expert")
    n_y, n_e = lax.axis_size("dp") // 2, lax.axis_size("expert")
    y, c = lax.div(dp, 2), lax.rem(dp, 2)
    other = 1 - c
    partner = (2 * y + other, e)
    chip = lambda d: lax.rem(y + d + n_y, n_y)
    line = lambda d: (2 * chip(d) + c, e)
    plane = lambda d: (dp, lax.rem(e + d, n_e))

    def remote(src, dst, send, recv, device):
        return pltpu.make_async_remote_copy(src, dst, send, recv, device_id=device, device_id_type=MESH)

    barrier = pltpu.get_barrier_semaphore()

    def greet(device):
        pl.semaphore_signal(barrier, inc=1, device_id=device, device_id_type=MESH)

    greet(partner)
    lax.fori_loop(1, n_y, lambda d, _: (greet(line(d)), 0)[1], 0)
    lax.fori_loop(1, n_e, lambda d, _: (greet(plane(d)), 0)[1], 0)
    pl.semaphore_wait(barrier, n_y + n_e - 1)

    depth, half = gate_ref.shape[0], gate_ref.shape[1] // 2
    mine = pl.ds(pl.multiple_of(c * half, 128), half)
    theirs = pl.ds(pl.multiple_of(other * half, 128), half)
    at = pl.ds(pl.multiple_of(c * depth, depth), depth)
    swaps = [
        remote(ref.at[:, theirs], weights.at[y, g, at], swap_send.at[g], swap_recv.at[g], partner)
        for g, ref in enumerate((gate_ref, up_ref))
    ]
    owns = [
        pltpu.make_async_copy(ref.at[:, mine], weights.at[y, g, at], own_sem.at[g])
        for g, ref in enumerate((gate_ref, up_ref))
    ]
    for copy in swaps + owns:
        copy.start()

    def token_copy(d):
        return remote(
            outgoing_ref.at[lax.rem(e + d, n_e)], tok.at[c, e], tok_send.at[d], tok_recv.at[e], plane(d)
        )

    own_tokens = pltpu.make_async_copy(outgoing_ref.at[e], tok.at[c, e], own_sem.at[2])
    own_tokens.start()
    lax.fori_loop(1, n_e, lambda d, _: (token_copy(d).start(), 0)[1], 0)

    steps = n_y // 2

    def ring(way, step, g, origin):
        k = (1 - way) // 2
        b = chip(-way * (step - 1 + origin))
        return remote(
            weights.at[b, g], weights.at[b, g], ring_send.at[k, step - 1, g], ring_recv.at[k, step - 1, g], line(way)
        )

    def lanes(step):
        return [(1, 0), (-1, 1)] if step == steps else [(1, 0), (-1, 0), (1, 1), (-1, 1)]

    for g in range(2):
        owns[g].wait()
        swaps[g].wait_recv()
        for way, kind in lanes(1):
            if kind == g:
                ring(way, 1, g, 0).start()

    def arrive(step):
        for way, g in lanes(step):
            ring(way, step, g, 1).wait_recv()
            if step < steps and (way, g) in lanes(step + 1):
                ring(way, step + 1, g, 0).start()

    def multiply(b, g, first=False):
        columns = pl.ds(pl.multiple_of(b * 2 * depth, 2 * depth), 2 * depth)
        product = jnp.dot(rows[:, columns], weights[b, g], preferred_element_type=F32)
        if first:
            sums[g] = product
        else:
            sums[g] += product

    group = n_e // pass_send.shape[0]

    def token_pass(k):
        span = pl.ds(k * group, group)
        return remote(tok.at[c, span], tok.at[c, span], pass_send.at[k], pass_recv.at[k], partner)

    def token_in(k):
        span = pl.ds(k * group, group)
        return remote(tok.at[other, span], tok.at[other, span], pass_send.at[k], pass_recv.at[k], partner)

    def wait_token(source, carry):
        @pl.when(source == e)
        def _():
            own_tokens.wait()

        @pl.when(source != e)
        def _():
            remote(
                outgoing_ref.at[e], tok.at[c, source], tok_send.at[0], tok_recv.at[source], plane(0)
            ).wait_recv()

        return carry

    def settle(k, p):
        pair = jnp.concatenate([tok[k, 2 * p].astype(F32), tok[k, 2 * p + 1].astype(F32)], axis=0)
        rows[pl.ds(pl.multiple_of(k * n_e * 8 + p * 16, 16), 16), :] = pair.astype(BF16)

    arrived_before = max(1, steps - 2)
    for step in range(1, arrived_before + 1):
        arrive(step)
    for k in range(pass_send.shape[0]):
        lax.fori_loop(k * group, (k + 1) * group, wait_token, 0)
        token_pass(k).start()
    lax.fori_loop(0, n_e // 2, lambda p, _: (settle(c, p), 0)[1], 0)
    if arrived_before + 1 < steps:
        arrive(arrived_before + 1)
    for k in range(pass_send.shape[0]):
        token_in(k).wait_recv()
    lax.fori_loop(0, n_e // 2, lambda p, _: (settle(other, p), 0)[1], 0)
    for g in range(2):
        multiply(y, g, True)
    for step in range(1, steps):
        if step > arrived_before + 1:
            arrive(step)
        for way in (1, -1):
            for g in range(2):
                multiply(chip(-way * step), g)
    if steps > arrived_before:
        arrive(steps)
    for g in range(2):
        multiply(chip(steps), g)

    gate_sum, up_sum = sums[0], sums[1]
    hid[c] = (gate_sum / (1.0 + jnp.exp(-gate_sum)) * up_sum).astype(BF16)
    hid_out = remote(hid.at[c], hid.at[c], hid_send.at[0], hid_recv.at[0], partner)
    hid_out.start()
    remote(hid.at[other], hid.at[other], hid_send.at[0], hid_recv.at[0], partner).wait_recv()

    per_half = half // B
    for i in range(N // B):
        left = hid[i // per_half, :, (i % per_half) * B:(i % per_half + 1) * B]
        for h in range(i // per_half, 2):
            first = i % per_half if h == i // per_half else 0
            product = lax.dot_general(
                left, hid[h, :, first * B:], (TN, ((), ())), preferred_element_type=F32
            )
            for j in range(per_half - first):
                strips[:, block_at(i, h * per_half + first + j)] = product[:, j * B:(j + 1) * B].reshape(16, 8, B)

    def part_copy(d):
        return remote(strips.at[2 * chip(d) + c], parts.at[y], part_send.at[d], part_recv.at[y], line(d))

    lax.fori_loop(1, n_y, lambda d, _: (part_copy(d).start(), 0)[1], 0)
    gram_ref[dp] = strips[dp]

    def take_part(d, carry):
        source = chip(d)
        remote(strips.at[dp], parts.at[source], part_send.at[0], part_recv.at[source], line(0)).wait_recv()
        gram_ref[dp] += parts[source]
        return carry

    lax.fori_loop(1, n_y, take_part, 0)

    def share(owner, d, device):
        return remote(gram_ref.at[owner], gram_ref.at[owner], share_send.at[d], share_recv.at[owner], device)

    lax.fori_loop(1, n_y, lambda d, _: (share(dp, d, line(d)).start(), 0)[1], 0)
    share(dp, 0, partner).start()

    def hand_over(d, carry):
        owner = 2 * chip(d) + c
        share(owner, 0, partner).wait_recv()
        share(owner, n_y + d, partner).start()
        return carry

    lax.fori_loop(1, n_y, hand_over, 0)
    lax.fori_loop(0, n_y, lambda d, _: (share(2 * chip(d) + other, 0, partner).wait_recv(), 0)[1], 0)

    for copy in swaps:
        copy.wait_send()
    lax.fori_loop(1, n_e, lambda d, _: (token_copy(d).wait_send(), 0)[1], 0)
    for k in range(pass_send.shape[0]):
        token_pass(k).wait_send()
    for step in range(1, steps + 1):
        for way, g in lanes(step):
            ring(way, step, g, 0).wait_send()
    hid_out.wait_send()
    lax.fori_loop(1, n_y, lambda d, _: (part_copy(d).wait_send(), 0)[1], 0)
    share(dp, 0, partner).wait_send()
    lax.fori_loop(1, n_y, lambda d, _: (share(dp, d, line(d)).wait_send(), 0)[1], 0)
    lax.fori_loop(1, n_y, lambda d, _: (share(2 * chip(d) + c, n_y + d, partner).wait_send(), 0)[1], 0)


def exchange_call(outgoing, gate, up):
    n_e, slots, width = outgoing.shape
    n_dp = lax.axis_size("dp")
    n_y, depth, half = n_dp // 2, gate.shape[0], gate.shape[1] // 2
    count = (N // B) * (N // B + 1) // 2
    groups = 4
    dma = lambda *shape: pltpu.SemaphoreType.DMA(shape)
    vmem = pl.BlockSpec(memory_space=pltpu.VMEM)
    return pl.pallas_call(
        exchange_kernel,
        out_shape=jax.ShapeDtypeStruct((n_dp, count, 8, B), F32),
        in_specs=[vmem] * 3,
        out_specs=vmem,
        scratch_shapes=[
            pltpu.VMEM((2, n_e, slots, width), BF16),
            pltpu.VMEM((2 * n_e * slots, width), BF16),
            pltpu.VMEM((n_y, 2, 2 * depth, half), BF16),
            pltpu.VMEM((2, 2 * n_e * slots, half), F32),
            pltpu.VMEM((2, 2 * n_e * slots, half), BF16),
            pltpu.VMEM((n_dp, count, 8, B), F32),
            pltpu.VMEM((n_y, count, 8, B), F32),
            dma(3), dma(2), dma(2), dma(n_e), dma(n_e), dma(groups), dma(groups),
            dma(2, n_y // 2, 2), dma(2, n_y // 2, 2), dma(1), dma(1), dma(n_y), dma(n_y), dma(2 * n_y), dma(n_dp),
        ],
        compiler_params=pltpu.CompilerParams(
            collective_id=0, has_side_effects=True, vmem_limit_bytes=48 << 20
        ),
    )(outgoing, gate, up)


def body(tokens, expert_ids, gate_weight, up_weight, down_weight):
    owners = lax.axis_size("expert")
    tok_rows = tokens.shape[0]
    expert_range = jnp.arange(owners, dtype=jnp.int32)
    member = jnp.any(expert_ids[:, :, None] == expert_range[None, None, :], axis=1)
    earlier = (jnp.arange(tok_rows)[:, None] > jnp.arange(tok_rows)[None, :]).astype(jnp.int32)
    ranking = jnp.dot(earlier, member.astype(jnp.int32))
    slot_range = jnp.arange(CAP, dtype=jnp.int32)
    placing = (member[:, :, None] & (ranking[:, :, None] == slot_range[None, None, :])).astype(BF16)
    outgoing = jnp.einsum("tec,td->ecd", placing, tokens, preferred_element_type=F32).astype(BF16)
    gram = exchange_call(outgoing, gate_weight[0], up_weight[0])
    place = lax.axis_index("dp").astype(jnp.int32).reshape(1)
    own_rows, whitened = local_call(place, gram, down_weight[0], N // lax.axis_size("dp"))
    return (own_rows[None], whitened[None])


def solution(mesh):
    return jax.shard_map(
        body,
        mesh=mesh,
        in_specs=(
            P(("dp", "expert"), None),
            P(("dp", "expert"), None),
            P("expert", "dp", None),
            P("expert", "dp", None),
            P("expert", None, "dp"),
        ),
        out_specs=(P("expert", "dp", None), P("expert", None, "dp")),
        check_vma=False,
    )
```

```python
import jax
import jax.numpy as jnp
from jax import lax
from jax.experimental import pallas as pl
from jax.experimental.pallas import tpu as pltpu
from jax.sharding import PartitionSpec as P

F32, BF16 = jnp.float32, jnp.bfloat16
N, B, H = 768, 128, 64
CAP = 8
SLOTS = 256
damping = 0.02


def split(x):
    high = x.astype(BF16)
    return high, (x - high.astype(F32)).astype(BF16)


def dot3(left, right, dims):
    lh, ll = split(left)
    rh, rl = split(right)
    dot = lambda a, b: lax.dot_general(a, b, (dims, ((), ())), preferred_element_type=F32)
    return dot(lh, rh) + (dot(lh, rl) + dot(ll, rh))


NN, TN = ((1,), (0,)), ((0,), (0,))


def eliminate(rows8, first):
    tiles = list(rows8)
    sublane = lax.broadcasted_iota(jnp.int32, (8, 128), 0)
    lane_copy = lambda x, c: jnp.broadcast_to(x[:, c:c + 1], (8, 128))
    row_copy = lambda x, i: jnp.broadcast_to(x[i:i + 1, :], (8, 128))
    columns = [lane_copy(tiles[0], first + j) for j in range(8)]
    for s in range(8):
        base = first + 8 * s
        ahead = [lane_copy(tiles[s + 1], base + 8 + j) for j in range(8)] if s < 7 else []
        a = {(i, j): row_copy(columns[j], i) for j in range(8) for i in range(j, 8)}
        row = [row_copy(tiles[s], j) for j in range(8)]
        inv, low = [], {}
        for j in range(8):
            r = lax.rsqrt(a[j, j])
            inv.append(r)
            for i in range(j + 1, 8):
                low[i, j] = a[i, j] * r
            for jj in range(j + 1, 8):
                for i in range(jj, 8):
                    a[i, jj] = a[i, jj] - low[i, j] * low[jj, j]
            row[j] = row[j] * r
            for i in range(j + 1, 8):
                row[i] = row[i] - low[i, j] * row[j]
        for t in range(s + 1, 8):
            column = [lane_copy(tiles[t], base + j) for j in range(8)]
            total = tiles[t]
            for j in range(8):
                column[j] = column[j] * inv[j]
                for jj in range(j + 1, 8):
                    column[jj] = column[jj] - column[j] * low[jj, j]
                total = total - column[j] * row[j]
                if t == s + 1:
                    ahead = [ahead[k] - column[j] * row_copy(column[j], k) for k in range(8)]
            tiles[t] = total
        columns = ahead
        done = row[0]
        for j in range(1, 8):
            done = jnp.where(sublane == j, row[j], done)
        tiles[s] = done
    return jnp.concatenate(tiles, axis=0)


def factor_block(block):
    lane = lax.broadcasted_iota(jnp.int32, (H, B), 1)
    row = lax.broadcasted_iota(jnp.int32, (H, B), 0)
    zero = jnp.zeros((H, B), F32)
    top, bottom = block[:H], block[H:]
    work = jnp.where(lane < H, top, jnp.where(lane == row + H, 1.0, 0.0))
    done0 = eliminate([work[8 * t:8 * t + 8] for t in range(8)], 0)
    inv0 = jnp.where(lane < H, 0.0, done0)
    upper0 = dot3(inv0, jnp.concatenate([zero, top], axis=0), NN)
    upper0 = jnp.where(lane < H, jnp.where(lane >= row, done0, 0.0), upper0)
    bottom = bottom - dot3(upper0, upper0, TN)[H:]
    mixed = dot3(upper0, inv0, TN)[H:]
    work = jnp.where(lane >= H, bottom, jnp.where(lane == row, 1.0, 0.0))
    done1 = eliminate([work[8 * t:8 * t + 8] for t in range(8)], H)
    upper1 = jnp.where(lane >= row + H, done1, 0.0)
    inv1 = jnp.where(lane < H, done1, 0.0)
    inv1 = inv1 - dot3(inv1, jnp.concatenate([mixed, zero], axis=0), NN)
    return jnp.concatenate([upper0, upper1], axis=0), jnp.concatenate([inv0, inv1], axis=0)


def factor_all(work_ref):
    count = N // B

    def step(q, carry):
        here = pl.ds(pl.multiple_of(q * B, B), B)
        upper, inverse = factor_block(work_ref[here, here])
        work_ref[here, here] = upper
        for static in range(count - 1):
            @pl.when(q == static)
            def _(static=static):
                own, after = slice(static * B, static * B + B), slice(static * B + B, N)
                strip = work_ref[own, after]
                strip = jnp.concatenate([strip[H:], strip[:H]], axis=0)
                strip = dot3(inverse, strip, NN)
                work_ref[own, after] = strip
                high, low = split(strip)
                dot = lambda a, b: lax.dot_general(a, b, (TN, ((), ())), preferred_element_type=F32)
                for i in range(static + 1, count):
                    at = (i - static - 1) * B
                    lh, ll, rh, rl = high[:, at:at + B], low[:, at:at + B], high[:, at:], low[:, at:]
                    work_ref[i * B:i * B + B, i * B:] -= dot(lh, rh) + (dot(lh, rl) + dot(ll, rh))
        return carry

    lax.fori_loop(0, count, step, 0)


def whiten(work_ref, down_ref, white_ref):
    for q in range(N // B):
        own = slice(q * B, q * B + B)
        high, low = split(work_ref[own, q * B:])
        down = down_ref[q * B:, :]
        white_ref[own, :] = jnp.dot(high, down, preferred_element_type=F32) + jnp.dot(low, down, preferred_element_type=F32)


def local_kernel(place_ref, gram_ref, down_ref, rows_ref, white_ref, work_ref):
    diagonal = lax.broadcasted_iota(jnp.int32, (B, B), 0) == lax.broadcasted_iota(jnp.int32, (B, B), 1)
    for i in range(N // B):
        for j in range(i, N // B):
            block = gram_ref[:, block_at(i, j)].reshape(B, B) * (1.0 / SLOTS)
            if i == j:
                block = block + jnp.where(diagonal, damping, 0.0)
            work_ref[i * B:i * B + B, j * B:j * B + B] = block
        if i:
            work_ref[i * B:i * B + B, :i * B] = jnp.zeros((B, i * B), F32)
    factor_all(work_ref)
    share = rows_ref.shape[0]
    rows_ref[...] = work_ref[pl.ds(pl.multiple_of(place_ref[0] * share, 8), share), :]
    whiten(work_ref, down_ref, white_ref)


def local_call(place, gram, down, share=48):
    vmem = pl.BlockSpec(memory_space=pltpu.VMEM)
    return pl.pallas_call(
        local_kernel,
        out_shape=(jax.ShapeDtypeStruct((share, N), F32), jax.ShapeDtypeStruct((N, down.shape[1]), F32)),
        in_specs=[pl.BlockSpec(memory_space=pltpu.SMEM), vmem, vmem],
        out_specs=(vmem, vmem),
        scratch_shapes=[pltpu.VMEM((N, N), F32)],
        compiler_params=pltpu.CompilerParams(vmem_limit_bytes=48 << 20),
    )(place, gram, down)


MESH = pl.DeviceIdType.MESH


def block_at(i, j):
    return i * (N // B) - i * (i - 1) // 2 + j - i


def exchange_kernel(
    outgoing_ref, gate_ref, up_ref, gram_ref, tok, rows, weights, sums, hid, strips, parts,
    own_sem, swap_send, swap_recv, tok_send, tok_recv, pass_send, pass_recv, first_send, first_recv, ring_send, ring_recv,
    hid_send, hid_recv, part_send, part_recv, share_send, share_recv, hand_send, hand_recv,
):
    dp, e = lax.axis_index("dp"), lax.axis_index("expert")
    n_y, n_e = lax.axis_size("dp") // 2, lax.axis_size("expert")
    y, c = lax.div(dp, 2), lax.rem(dp, 2)
    other = 1 - c
    partner = (2 * y + other, e)
    chip = lambda d: lax.rem(y + d + n_y, n_y)
    line = lambda d: (2 * chip(d) + c, e)
    plane = lambda d: (dp, lax.rem(e + d, n_e))

    def remote(src, dst, send, recv, device):
        return pltpu.make_async_remote_copy(src, dst, send, recv, device_id=device, device_id_type=MESH)

    barrier = pltpu.get_barrier_semaphore()

    def greet(device):
        pl.semaphore_signal(barrier, inc=1, device_id=device, device_id_type=MESH)

    greet(partner)
    lax.fori_loop(1, n_y, lambda d, _: (greet(line(d)), 0)[1], 0)
    for way in (1, -1):
        greet((2 * chip(way) + other, e))
    lax.fori_loop(1, n_e, lambda d, _: (greet(plane(d)), 0)[1], 0)
    pl.semaphore_wait(barrier, n_y + n_e + 1)

    depth, half = gate_ref.shape[0], gate_ref.shape[1] // 2
    steps = n_y // 2
    mine = pl.ds(pl.multiple_of(c * half, 128), half)
    theirs = pl.ds(pl.multiple_of(other * half, 128), half)
    at = pl.ds(pl.multiple_of(c * depth, depth), depth)
    sources = (gate_ref, up_ref)

    def first(way, g, same):
        k = (1 - way) // 2
        return remote(
            sources[g].at[:, mine if same else theirs], weights.at[y, g, at],
            first_send.at[k, g, 0 if same else 1], first_recv.at[k, g, c],
            (2 * chip(way) + (c if same else other), e),
        )

    def first_in(way, g, source):
        k = (1 - way) // 2
        part = pl.ds(source * depth, depth)
        return remote(
            sources[g].at[:, mine], weights.at[chip(-way), g, part],
            first_send.at[k, g, 0], first_recv.at[k, g, source], line(way),
        )

    for g in range(2):
        for way in (1, -1):
            for same in (True, False):
                first(way, g, same).start()
    swaps = [
        remote(ref.at[:, theirs], weights.at[y, g, at], swap_send.at[g], swap_recv.at[g], partner)
        for g, ref in enumerate(sources)
    ]
    owns = [
        pltpu.make_async_copy(ref.at[:, mine], weights.at[y, g, at], own_sem.at[g])
        for g, ref in enumerate(sources)
    ]
    for copy in swaps + owns:
        copy.start()

    def token_copy(d):
        return remote(
            outgoing_ref.at[lax.rem(e + d, n_e)], tok.at[c, e], tok_send.at[d], tok_recv.at[e], plane(d)
        )

    own_tokens = pltpu.make_async_copy(outgoing_ref.at[e], tok.at[c, e], own_sem.at[2])
    own_tokens.start()
    lax.fori_loop(1, n_e, lambda d, _: (token_copy(d).start(), 0)[1], 0)

    def ring(way, step, g, origin):
        k = (1 - way) // 2
        b = chip(-way * (step - 1 + origin))
        return remote(
            weights.at[b, g], weights.at[b, g], ring_send.at[k, step - 2, g], ring_recv.at[k, step - 2, g], line(way)
        )

    def lanes(step):
        return [(1, 0), (-1, 1)] if step == steps else [(1, 0), (-1, 0), (1, 1), (-1, 1)]

    def arrive(step):
        for way, g in lanes(step):
            if step == 1:
                for source in range(2):
                    first_in(way, g, source).wait_recv()
            else:
                ring(way, step, g, 1).wait_recv()
            if step < steps and (way, g) in lanes(step + 1):
                ring(way, step + 1, g, 0).start()

    def multiply(b, g, first=False):
        columns = pl.ds(pl.multiple_of(b * 2 * depth, 2 * depth), 2 * depth)
        product = jnp.dot(rows[:, columns], weights[b, g], preferred_element_type=F32)
        if first:
            sums[g] = product
        else:
            sums[g] += product

    group = n_e // pass_send.shape[0]

    def token_pass(k):
        span = pl.ds(k * group, group)
        return remote(tok.at[c, span], tok.at[c, span], pass_send.at[k], pass_recv.at[k], partner)

    def token_in(k):
        span = pl.ds(k * group, group)
        return remote(tok.at[other, span], tok.at[other, span], pass_send.at[k], pass_recv.at[k], partner)

    def wait_token(source, carry):
        @pl.when(source == e)
        def _():
            own_tokens.wait()

        @pl.when(source != e)
        def _():
            remote(
                outgoing_ref.at[e], tok.at[c, source], tok_send.at[0], tok_recv.at[source], plane(0)
            ).wait_recv()

        return carry

    def settle(k, p):
        pair = jnp.concatenate([tok[k, 2 * p].astype(F32), tok[k, 2 * p + 1].astype(F32)], axis=0)
        rows[pl.ds(pl.multiple_of(k * n_e * 8 + p * 16, 16), 16), :] = pair.astype(BF16)

    arrived_before = max(1, steps - 2)
    for step in range(1, arrived_before + 1):
        arrive(step)
    for k in range(pass_send.shape[0]):
        lax.fori_loop(k * group, (k + 1) * group, wait_token, 0)
        token_pass(k).start()
    lax.fori_loop(0, n_e // 2, lambda p, _: (settle(c, p), 0)[1], 0)
    if arrived_before + 1 < steps:
        arrive(arrived_before + 1)
    for k in range(pass_send.shape[0]):
        token_in(k).wait_recv()
    lax.fori_loop(0, n_e // 2, lambda p, _: (settle(other, p), 0)[1], 0)
    for g in range(2):
        owns[g].wait()
        swaps[g].wait_recv()
        multiply(y, g, True)
    for step in range(1, steps):
        if step > arrived_before + 1:
            arrive(step)
        for way in (1, -1):
            for g in range(2):
                multiply(chip(-way * step), g)
    if steps > arrived_before:
        arrive(steps)
    for g in range(2):
        multiply(chip(steps), g)

    gate_sum, up_sum = sums[0], sums[1]
    hid[c] = (gate_sum / (1.0 + jnp.exp(-gate_sum)) * up_sum).astype(BF16)
    hid_out = remote(hid.at[c], hid.at[c], hid_send.at[0], hid_recv.at[0], partner)
    hid_out.start()
    remote(hid.at[other], hid.at[other], hid_send.at[0], hid_recv.at[0], partner).wait_recv()

    per_half = half // B
    for i in range(N // B):
        left = hid[i // per_half, :, (i % per_half) * B:(i % per_half + 1) * B]
        for h in range(i // per_half, 2):
            begin = i % per_half if h == i // per_half else 0
            product = lax.dot_general(
                left, hid[h, :, begin * B:], (TN, ((), ())), preferred_element_type=F32
            )
            for j in range(per_half - begin):
                strips[:, block_at(i, h * per_half + begin + j)] = product[:, j * B:(j + 1) * B].reshape(16, 8, B)

    count = strips.shape[1]
    cut = (count + 1) // 2
    pieces = (pl.ds(0, cut), pl.ds(cut, count - cut))
    flows = [(0, 1), (1, -1), (0, -1), (1, 1)]

    def hops(piece, way):
        return steps if way == (1, -1)[piece] else steps - 1

    def part(piece, way, step, origin):
        k = (1 - way) // 2
        owner = chip(way * (hops(piece, way) + 1 - step) - way * origin)
        return remote(
            strips.at[2 * owner + c, pieces[piece]], parts.at[k, step - 1, pieces[piece]],
            part_send.at[k, step - 1, piece], part_recv.at[k, step - 1, piece], line(way),
        )

    for step in range(1, steps + 1):
        for piece, way in flows:
            if step <= hops(piece, way):
                if step > 1:
                    k, owner = (1 - way) // 2, chip(way * (hops(piece, way) + 1 - step))
                    part(piece, way, step - 1, 1).wait_recv()
                    strips[2 * owner + c, pieces[piece]] += parts[k, step - 2, pieces[piece]]
                part(piece, way, step, 0).start()

    def share(piece, way, step, origin):
        k = (1 - way) // 2
        strip = gram_ref.at[2 * chip(-way * (step - 1 + origin)) + c, pieces[piece]]
        return remote(
            strip, strip, share_send.at[k, step - 1, piece], share_recv.at[k, step - 1, piece], line(way)
        )

    def hand(piece, d, core):
        strip = gram_ref.at[2 * chip(d) + core, pieces[piece]]
        return remote(strip, strip, hand_send.at[d % n_y, piece], hand_recv.at[d % n_y, piece], partner)

    for piece in range(2):
        total = strips[dp, pieces[piece]]
        for way in (1, -1):
            last = hops(piece, way)
            part(piece, way, last, 1).wait_recv()
            total = total + parts[(1 - way) // 2, last - 1, pieces[piece]]
        gram_ref[dp, pieces[piece]] = total
        for way in (1, -1):
            share(piece, way, 1, 0).start()
        hand(piece, 0, c).start()
    for step in range(1, steps + 1):
        for piece, way in flows:
            if step <= hops(piece, way):
                share(piece, way, step, 1).wait_recv()
                if step < hops(piece, way):
                    share(piece, way, step + 1, 0).start()
                hand(piece, -way * step, c).start()
    for d in range(n_y):
        for piece in range(2):
            hand(piece, d, other).wait_recv()

    for copy in swaps:
        copy.wait_send()
    for g in range(2):
        for way in (1, -1):
            for same in (True, False):
                first(way, g, same).wait_send()
    lax.fori_loop(1, n_e, lambda d, _: (token_copy(d).wait_send(), 0)[1], 0)
    for k in range(pass_send.shape[0]):
        token_pass(k).wait_send()
    for step in range(2, steps + 1):
        for way, g in lanes(step):
            ring(way, step, g, 0).wait_send()
    hid_out.wait_send()
    for step in range(1, steps + 1):
        for piece, way in flows:
            if step <= hops(piece, way):
                part(piece, way, step, 0).wait_send()
                share(piece, way, step, 0).wait_send()
    for d in range(n_y):
        for piece in range(2):
            hand(piece, d, c).wait_send()


def exchange_call(outgoing, gate, up):
    n_e, slots, width = outgoing.shape
    n_dp = lax.axis_size("dp")
    n_y, depth, half = n_dp // 2, gate.shape[0], gate.shape[1] // 2
    count = (N // B) * (N // B + 1) // 2
    groups, steps = 4, n_y // 2
    dma = lambda *shape: pltpu.SemaphoreType.DMA(shape)
    vmem = pl.BlockSpec(memory_space=pltpu.VMEM)
    return pl.pallas_call(
        exchange_kernel,
        out_shape=jax.ShapeDtypeStruct((n_dp, count, 8, B), F32),
        in_specs=[vmem] * 3,
        out_specs=vmem,
        scratch_shapes=[
            pltpu.VMEM((2, n_e, slots, width), BF16),
            pltpu.VMEM((2 * n_e * slots, width), BF16),
            pltpu.VMEM((n_y, 2, 2 * depth, half), BF16),
            pltpu.VMEM((2, 2 * n_e * slots, half), F32),
            pltpu.VMEM((2, 2 * n_e * slots, half), BF16),
            pltpu.VMEM((n_dp, count, 8, B), F32),
            pltpu.VMEM((2, n_y // 2, count, 8, B), F32),
            dma(3), dma(2), dma(2), dma(n_e), dma(n_e), dma(groups), dma(groups), dma(2, 2, 2), dma(2, 2, 2),
            dma(2, steps - 1, 2), dma(2, steps - 1, 2), dma(1), dma(1),
            dma(2, steps, 2), dma(2, steps, 2), dma(2, steps, 2), dma(2, steps, 2), dma(n_y, 2), dma(n_y, 2),
        ],
        compiler_params=pltpu.CompilerParams(
            collective_id=0, has_side_effects=True, vmem_limit_bytes=48 << 20
        ),
    )(outgoing, gate, up)


def body(tokens, expert_ids, gate_weight, up_weight, down_weight):
    owners = lax.axis_size("expert")
    tok_rows = tokens.shape[0]
    expert_range = jnp.arange(owners, dtype=jnp.int32)
    member = jnp.any(expert_ids[:, :, None] == expert_range[None, None, :], axis=1)
    earlier = (jnp.arange(tok_rows)[:, None] > jnp.arange(tok_rows)[None, :]).astype(jnp.int32)
    ranking = jnp.dot(earlier, member.astype(jnp.int32))
    slot_range = jnp.arange(CAP, dtype=jnp.int32)
    placing = (member[:, :, None] & (ranking[:, :, None] == slot_range[None, None, :])).astype(BF16)
    outgoing = jnp.einsum("tec,td->ecd", placing, tokens, preferred_element_type=F32).astype(BF16)
    gram = exchange_call(outgoing, gate_weight[0], up_weight[0])
    place = lax.axis_index("dp").astype(jnp.int32).reshape(1)
    own_rows, whitened = local_call(place, gram, down_weight[0], N // lax.axis_size("dp"))
    return (own_rows[None], whitened[None])


def solution(mesh):
    return jax.shard_map(
        body,
        mesh=mesh,
        in_specs=(
            P(("dp", "expert"), None),
            P(("dp", "expert"), None),
            P("expert", "dp", None),
            P("expert", "dp", None),
            P("expert", None, "dp"),
        ),
        out_specs=(P("expert", "dp", None), P("expert", None, "dp")),
        check_vma=False,
    )
```

```python
import jax
import jax.numpy as jnp
from jax import lax
from jax.experimental import pallas as pl
from jax.experimental.pallas import tpu as pltpu
from jax.sharding import PartitionSpec as P

F32, BF16 = jnp.float32, jnp.bfloat16
N, B, H = 768, 128, 64
CAP = 8
SLOTS = 256
damping = 0.02


def split(x):
    high = x.astype(BF16)
    return high, (x - high.astype(F32)).astype(BF16)


def dot3(left, right, dims):
    lh, ll = split(left)
    rh, rl = split(right)
    dot = lambda a, b: lax.dot_general(a, b, (dims, ((), ())), preferred_element_type=F32)
    return dot(lh, rh) + (dot(lh, rl) + dot(ll, rh))


NN, TN = ((1,), (0,)), ((0,), (0,))


def eliminate(rows8, first):
    tiles = list(rows8)
    sublane = lax.broadcasted_iota(jnp.int32, (8, 128), 0)
    lane_copy = lambda x, c: jnp.broadcast_to(x[:, c:c + 1], (8, 128))
    row_copy = lambda x, i: jnp.broadcast_to(x[i:i + 1, :], (8, 128))
    columns = [lane_copy(tiles[0], first + j) for j in range(8)]
    for s in range(8):
        base = first + 8 * s
        ahead = [lane_copy(tiles[s + 1], base + 8 + j) for j in range(8)] if s < 7 else []
        a = {(i, j): row_copy(columns[j], i) for j in range(8) for i in range(j, 8)}
        row = [row_copy(tiles[s], j) for j in range(8)]
        inv, low = [], {}
        for j in range(8):
            r = lax.rsqrt(a[j, j])
            inv.append(r)
            for i in range(j + 1, 8):
                low[i, j] = a[i, j] * r
            for jj in range(j + 1, 8):
                for i in range(jj, 8):
                    a[i, jj] = a[i, jj] - low[i, j] * low[jj, j]
            row[j] = row[j] * r
            for i in range(j + 1, 8):
                row[i] = row[i] - low[i, j] * row[j]
        for t in range(s + 1, 8):
            column = [lane_copy(tiles[t], base + j) for j in range(8)]
            total = tiles[t]
            for j in range(8):
                column[j] = column[j] * inv[j]
                for jj in range(j + 1, 8):
                    column[jj] = column[jj] - column[j] * low[jj, j]
                total = total - column[j] * row[j]
                if t == s + 1:
                    ahead = [ahead[k] - column[j] * row_copy(column[j], k) for k in range(8)]
            tiles[t] = total
        columns = ahead
        done = row[0]
        for j in range(1, 8):
            done = jnp.where(sublane == j, row[j], done)
        tiles[s] = done
    return jnp.concatenate(tiles, axis=0)


def factor_block(block):
    lane = lax.broadcasted_iota(jnp.int32, (H, B), 1)
    row = lax.broadcasted_iota(jnp.int32, (H, B), 0)
    zero = jnp.zeros((H, B), F32)
    top, bottom = block[:H], block[H:]
    work = jnp.where(lane < H, top, jnp.where(lane == row + H, 1.0, 0.0))
    done0 = eliminate([work[8 * t:8 * t + 8] for t in range(8)], 0)
    inv0 = jnp.where(lane < H, 0.0, done0)
    upper0 = dot3(inv0, jnp.concatenate([zero, top], axis=0), NN)
    upper0 = jnp.where(lane < H, jnp.where(lane >= row, done0, 0.0), upper0)
    bottom = bottom - dot3(upper0, upper0, TN)[H:]
    mixed = dot3(upper0, inv0, TN)[H:]
    work = jnp.where(lane >= H, bottom, jnp.where(lane == row, 1.0, 0.0))
    done1 = eliminate([work[8 * t:8 * t + 8] for t in range(8)], H)
    upper1 = jnp.where(lane >= row + H, done1, 0.0)
    inv1 = jnp.where(lane < H, done1, 0.0)
    inv1 = inv1 - dot3(inv1, jnp.concatenate([mixed, zero], axis=0), NN)
    return jnp.concatenate([upper0, upper1], axis=0), jnp.concatenate([inv0, inv1], axis=0)


def factor_all(work_ref):
    count = N // B

    def step(q, carry):
        here = pl.ds(pl.multiple_of(q * B, B), B)
        upper, inverse = factor_block(work_ref[here, here])
        work_ref[here, here] = upper
        for static in range(count - 1):
            @pl.when(q == static)
            def _(static=static):
                own, after = slice(static * B, static * B + B), slice(static * B + B, N)
                strip = work_ref[own, after]
                strip = jnp.concatenate([strip[H:], strip[:H]], axis=0)
                strip = dot3(inverse, strip, NN)
                work_ref[own, after] = strip
                high, low = split(strip)
                dot = lambda a, b: lax.dot_general(a, b, (TN, ((), ())), preferred_element_type=F32)
                for i in range(static + 1, count):
                    at = (i - static - 1) * B
                    lh, ll, rh, rl = high[:, at:at + B], low[:, at:at + B], high[:, at:], low[:, at:]
                    work_ref[i * B:i * B + B, i * B:] -= dot(lh, rh) + (dot(lh, rl) + dot(ll, rh))
        return carry

    lax.fori_loop(0, count, step, 0)


def whiten(work_ref, down_ref, white_ref):
    for q in range(N // B):
        own = slice(q * B, q * B + B)
        high, low = split(work_ref[own, q * B:])
        down = down_ref[q * B:, :]
        white_ref[own, :] = jnp.dot(high, down, preferred_element_type=F32) + jnp.dot(low, down, preferred_element_type=F32)


def local_kernel(place_ref, gram_ref, down_ref, rows_ref, white_ref, work_ref):
    diagonal = lax.broadcasted_iota(jnp.int32, (B, B), 0) == lax.broadcasted_iota(jnp.int32, (B, B), 1)
    for i in range(N // B):
        for j in range(i, N // B):
            block = gram_ref[:, block_at(i, j)].reshape(B, B) * (1.0 / SLOTS)
            if i == j:
                block = block + jnp.where(diagonal, damping, 0.0)
            work_ref[i * B:i * B + B, j * B:j * B + B] = block
        if i:
            work_ref[i * B:i * B + B, :i * B] = jnp.zeros((B, i * B), F32)
    factor_all(work_ref)
    share = rows_ref.shape[0]
    rows_ref[...] = work_ref[pl.ds(pl.multiple_of(place_ref[0] * share, 8), share), :]
    whiten(work_ref, down_ref, white_ref)


def local_call(place, gram, down, share=48):
    vmem = pl.BlockSpec(memory_space=pltpu.VMEM)
    return pl.pallas_call(
        local_kernel,
        out_shape=(jax.ShapeDtypeStruct((share, N), F32), jax.ShapeDtypeStruct((N, down.shape[1]), F32)),
        in_specs=[pl.BlockSpec(memory_space=pltpu.SMEM), vmem, vmem],
        out_specs=(vmem, vmem),
        scratch_shapes=[pltpu.VMEM((N, N), F32)],
        compiler_params=pltpu.CompilerParams(vmem_limit_bytes=48 << 20),
    )(place, gram, down)


MESH = pl.DeviceIdType.MESH
PIECES = 2


def block_at(i, j):
    return i * (N // B) - i * (i - 1) // 2 + j - i


def exchange_kernel(
    tokens_ref, ids_ref, gate_ref, up_ref, gram_ref, outgoing_ref, tokens, named, tok, rows, weights, sums, hid, strips, parts,
    own_sem, swap_send, swap_recv, tok_send, tok_recv, pass_send, pass_recv, first_send, first_recv, ring_send, ring_recv,
    hid_send, hid_recv, part_send, part_recv, share_send, share_recv, hand_send, hand_recv,
):
    dp, e = lax.axis_index("dp"), lax.axis_index("expert")
    n_y, n_e = lax.axis_size("dp") // 2, lax.axis_size("expert")
    y, c = lax.div(dp, 2), lax.rem(dp, 2)
    other = 1 - c
    partner = (2 * y + other, e)
    chip = lambda d: lax.rem(y + d + n_y, n_y)
    line = lambda d: (2 * chip(d) + c, e)
    plane = lambda d: (dp, lax.rem(e + d, n_e))

    def remote(src, dst, send, recv, device):
        return pltpu.make_async_remote_copy(src, dst, send, recv, device_id=device, device_id_type=MESH)

    token_load = pltpu.make_async_copy(tokens_ref, tokens, own_sem.at[3])
    token_load.start()
    name_load = pltpu.make_async_copy(ids_ref, named, own_sem.at[4])
    name_load.start()
    barrier = pltpu.get_barrier_semaphore()

    def greet(device):
        pl.semaphore_signal(barrier, inc=1, device_id=device, device_id_type=MESH)

    greet(partner)
    lax.fori_loop(1, n_y, lambda d, _: (greet(line(d)), 0)[1], 0)
    for way in (1, -1):
        greet((2 * chip(way) + other, e))
    lax.fori_loop(1, n_e, lambda d, _: (greet(plane(d)), 0)[1], 0)
    pl.semaphore_wait(barrier, n_y + n_e + 1)

    depth, half = gate_ref.shape[0], gate_ref.shape[1] // 2
    steps = n_y // 2
    mine = pl.ds(pl.multiple_of(c * half, 128), half)
    theirs = pl.ds(pl.multiple_of(other * half, 128), half)
    at = pl.ds(pl.multiple_of(c * depth, depth), depth)
    sources = (gate_ref, up_ref)

    def first(way, g, same):
        k = (1 - way) // 2
        return remote(
            sources[g].at[:, mine if same else theirs], weights.at[y, g, at],
            first_send.at[k, g, 0 if same else 1], first_recv.at[k, g, c],
            (2 * chip(way) + (c if same else other), e),
        )

    def first_in(way, g, source):
        k = (1 - way) // 2
        part = pl.ds(source * depth, depth)
        return remote(
            sources[g].at[:, mine], weights.at[chip(-way), g, part],
            first_send.at[k, g, 0], first_recv.at[k, g, source], line(way),
        )

    for g in range(2):
        for way in (1, -1):
            for same in (True, False):
                first(way, g, same).start()
    swaps = [
        remote(ref.at[:, theirs], weights.at[y, g, at], swap_send.at[g], swap_recv.at[g], partner)
        for g, ref in enumerate(sources)
    ]
    owns = [
        pltpu.make_async_copy(ref.at[:, mine], weights.at[y, g, at], own_sem.at[g])
        for g, ref in enumerate(sources)
    ]
    for copy in swaps + owns:
        copy.start()

    token_load.wait()
    name_load.wait()
    rows_here = tokens.shape[0]
    ids = named[...]
    expert = lax.broadcasted_iota(jnp.int32, (n_e, rows_here), 0)
    member = jnp.zeros((n_e, rows_here), F32)
    for k in range(ids.shape[0]):
        member = member + jnp.where(ids[k:k + 1] == expert, 1.0, 0.0)
    before = lax.broadcasted_iota(jnp.int32, (rows_here, rows_here), 0)
    after = lax.broadcasted_iota(jnp.int32, (rows_here, rows_here), 1)
    earlier = jnp.where(before < after, 1.0, 0.0).astype(BF16)
    rank = jnp.dot(member.astype(BF16), earlier, preferred_element_type=F32)
    place = jnp.where(member > 0.5, rank, -1.0)
    slot = lax.broadcasted_iota(jnp.int32, (CAP, rows_here), 0).astype(F32)
    placing = jnp.concatenate([jnp.where(place[i:i + 1] == slot, 1.0, 0.0) for i in range(n_e)], axis=0).astype(BF16)
    step_width = 512
    for start in range(0, tokens.shape[1], step_width):
        picked = jnp.dot(placing, tokens[:, start:start + step_width], preferred_element_type=F32)
        for i in range(n_e):
            outgoing_ref[i, :, start:start + step_width] = picked[i * CAP:(i + 1) * CAP].astype(BF16)

    def token_copy(d):
        return remote(
            outgoing_ref.at[lax.rem(e + d, n_e)], tok.at[c, e], tok_send.at[d], tok_recv.at[e], plane(d)
        )

    own_tokens = pltpu.make_async_copy(outgoing_ref.at[e], tok.at[c, e], own_sem.at[2])
    own_tokens.start()
    lax.fori_loop(1, n_e, lambda d, _: (token_copy(d).start(), 0)[1], 0)

    def ring(way, step, g, origin):
        k = (1 - way) // 2
        b = chip(-way * (step - 1 + origin))
        return remote(
            weights.at[b, g], weights.at[b, g], ring_send.at[k, step - 2, g], ring_recv.at[k, step - 2, g], line(way)
        )

    def lanes(step):
        return [(1, 0), (-1, 1)] if step == steps else [(1, 0), (-1, 0), (1, 1), (-1, 1)]

    def arrive(step):
        for way, g in lanes(step):
            if step == 1:
                for source in range(2):
                    first_in(way, g, source).wait_recv()
            else:
                ring(way, step, g, 1).wait_recv()
            if step < steps and (way, g) in lanes(step + 1):
                ring(way, step + 1, g, 0).start()

    def multiply(b, g, first=False):
        columns = pl.ds(pl.multiple_of(b * 2 * depth, 2 * depth), 2 * depth)
        product = jnp.dot(rows[:, columns], weights[b, g], preferred_element_type=F32)
        if first:
            sums[g] = product
        else:
            sums[g] += product

    group = n_e // pass_send.shape[0]

    def token_pass(k):
        span = pl.ds(k * group, group)
        return remote(tok.at[c, span], tok.at[c, span], pass_send.at[k], pass_recv.at[k], partner)

    def token_in(k):
        span = pl.ds(k * group, group)
        return remote(tok.at[other, span], tok.at[other, span], pass_send.at[k], pass_recv.at[k], partner)

    def wait_token(source, carry):
        @pl.when(source == e)
        def _():
            own_tokens.wait()

        @pl.when(source != e)
        def _():
            remote(
                outgoing_ref.at[e], tok.at[c, source], tok_send.at[0], tok_recv.at[source], plane(0)
            ).wait_recv()

        return carry

    def settle(k, p):
        pair = jnp.concatenate([tok[k, 2 * p].astype(F32), tok[k, 2 * p + 1].astype(F32)], axis=0)
        rows[pl.ds(pl.multiple_of(k * n_e * 8 + p * 16, 16), 16), :] = pair.astype(BF16)

    arrived_before = max(1, steps - 2)
    for step in range(1, arrived_before + 1):
        arrive(step)
    for k in range(pass_send.shape[0]):
        lax.fori_loop(k * group, (k + 1) * group, wait_token, 0)
        token_pass(k).start()
    lax.fori_loop(0, n_e // 2, lambda p, _: (settle(c, p), 0)[1], 0)
    if arrived_before + 1 < steps:
        arrive(arrived_before + 1)
    for k in range(pass_send.shape[0]):
        token_in(k).wait_recv()
    lax.fori_loop(0, n_e // 2, lambda p, _: (settle(other, p), 0)[1], 0)
    for g in range(2):
        owns[g].wait()
        swaps[g].wait_recv()
        multiply(y, g, True)
    for step in range(1, steps):
        if step > arrived_before + 1:
            arrive(step)
        for way in (1, -1):
            for g in range(2):
                multiply(chip(-way * step), g)
    if steps > arrived_before:
        arrive(steps)
    for g in range(2):
        multiply(chip(steps), g)

    gate_sum, up_sum = sums[0], sums[1]
    hid[c] = (gate_sum / (1.0 + jnp.exp(-gate_sum)) * up_sum).astype(BF16)
    hid_out = remote(hid.at[c], hid.at[c], hid_send.at[0], hid_recv.at[0], partner)
    hid_out.start()
    remote(hid.at[other], hid.at[other], hid_send.at[0], hid_recv.at[0], partner).wait_recv()

    per_half = half // B
    for i in range(N // B):
        left = hid[i // per_half, :, (i % per_half) * B:(i % per_half + 1) * B]
        for h in range(i // per_half, 2):
            begin = i % per_half if h == i // per_half else 0
            product = lax.dot_general(
                left, hid[h, :, begin * B:], (TN, ((), ())), preferred_element_type=F32
            )
            for j in range(per_half - begin):
                strips[:, block_at(i, h * per_half + begin + j)] = product[:, j * B:(j + 1) * B].reshape(16, 8, B)

    count = strips.shape[1]
    cuts = [count * p // PIECES for p in range(PIECES + 1)]
    pieces = [pl.ds(low, high - low) for low, high in zip(cuts, cuts[1:])]
    longest = [1 - 2 * (p % 2) for p in range(PIECES)]
    flows = [(p, way) for p in range(PIECES) for way in (longest[p], -longest[p])]

    def hops(piece, way):
        return steps if way == longest[piece] else steps - 1

    AHEAD, BESIDE, NEAR, JOINED = range(4)
    spans = {AHEAD: (4, 2), BESIDE: (3, 1), NEAR: (1, 1), JOINED: (2, 2)}

    def part(piece, way, kind):
        k, (reach, jump) = (1 - way) // 2, spans[kind]
        return remote(
            strips.at[2 * chip(way * reach) + c, pieces[piece]], parts.at[k, kind, pieces[piece]],
            part_send.at[k, kind, piece], part_recv.at[k, kind, piece], line(way * jump),
        )

    def kinds(piece, way):
        return [AHEAD, BESIDE] if hops(piece, way) == 4 else [BESIDE]

    for piece, way in flows:
        for kind in kinds(piece, way):
            part(piece, way, kind).start()
    for piece, way in flows:
        part(piece, way, NEAR).start()
    for piece, way in flows:
        k, total = (1 - way) // 2, strips[2 * chip(2 * way) + c, pieces[piece]]
        for kind in kinds(piece, way):
            part(piece, way, kind).wait_recv()
            total = total + parts[k, kind, pieces[piece]]
        strips[2 * chip(2 * way) + c, pieces[piece]] = total
        part(piece, way, JOINED).start()

    FIRST, SECOND, THIRD, FOURTH = range(4)
    routes = {FIRST: (0, 1), SECOND: (0, 2), THIRD: (-2, 1), FOURTH: (-2, 2)}

    def share(piece, way, kind, sending):
        k, (source, jump) = (1 - way) // 2, routes[kind]
        strip = gram_ref.at[2 * chip(way * source if sending else way * (source - jump)) + c, pieces[piece]]
        return remote(
            strip, strip, share_send.at[k, kind, piece], share_recv.at[k, kind, piece], line(way * jump)
        )

    def onward(piece, way):
        return [FOURTH, THIRD] if hops(piece, way) == 4 else [THIRD]

    def hand(piece, d, core):
        strip = gram_ref.at[2 * chip(d) + core, pieces[piece]]
        return remote(strip, strip, hand_send.at[d % n_y, piece], hand_recv.at[d % n_y, piece], partner)

    for piece in range(PIECES):
        total = strips[dp, pieces[piece]]
        for kind in (NEAR, JOINED):
            for way in (1, -1):
                part(piece, way, kind).wait_recv()
                total = total + parts[(1 - way) // 2, kind, pieces[piece]]
        gram_ref[dp, pieces[piece]] = total
        for kind in (SECOND, FIRST):
            for way in (1, -1):
                share(piece, way, kind, True).start()
        hand(piece, 0, c).start()
    for piece, way in flows:
        share(piece, way, SECOND, False).wait_recv()
        for kind in onward(piece, way):
            share(piece, way, kind, True).start()
        hand(piece, -2 * way, c).start()
    for piece, way in flows:
        share(piece, way, FIRST, False).wait_recv()
        hand(piece, -way, c).start()
    for piece, way in flows:
        for kind in onward(piece, way)[::-1]:
            share(piece, way, kind, False).wait_recv()
            hand(piece, -way * (3 if kind == THIRD else 4), c).start()
    for d in range(n_y):
        for piece in range(PIECES):
            hand(piece, d, other).wait_recv()

    for copy in swaps:
        copy.wait_send()
    for g in range(2):
        for way in (1, -1):
            for same in (True, False):
                first(way, g, same).wait_send()
    lax.fori_loop(1, n_e, lambda d, _: (token_copy(d).wait_send(), 0)[1], 0)
    for k in range(pass_send.shape[0]):
        token_pass(k).wait_send()
    for step in range(2, steps + 1):
        for way, g in lanes(step):
            ring(way, step, g, 0).wait_send()
    hid_out.wait_send()
    for piece, way in flows:
        for kind in kinds(piece, way) + [NEAR, JOINED]:
            part(piece, way, kind).wait_send()
        for kind in onward(piece, way) + [FIRST, SECOND]:
            share(piece, way, kind, True).wait_send()
    for d in range(n_y):
        for piece in range(PIECES):
            hand(piece, d, c).wait_send()


def exchange_call(tokens, expert_ids, gate, up):
    n_dp, n_e = lax.axis_size("dp"), lax.axis_size("expert")
    slots, width = CAP, tokens.shape[1]
    n_y, depth, half = n_dp // 2, gate.shape[0], gate.shape[1] // 2
    count = (N // B) * (N // B + 1) // 2
    groups, steps = 4, n_y // 2
    dma = lambda *shape: pltpu.SemaphoreType.DMA(shape)
    vmem, anywhere = pl.BlockSpec(memory_space=pltpu.VMEM), pl.BlockSpec(memory_space=pltpu.HBM)
    return pl.pallas_call(
        exchange_kernel,
        out_shape=jax.ShapeDtypeStruct((n_dp, count, 8, B), F32),
        in_specs=[anywhere] * 4,
        out_specs=vmem,
        scratch_shapes=[
            pltpu.VMEM((n_e, slots, width), BF16),
            pltpu.VMEM(tokens.shape, BF16),
            pltpu.VMEM(expert_ids.shape, jnp.int32),
            pltpu.VMEM((2, n_e, slots, width), BF16),
            pltpu.VMEM((2 * n_e * slots, width), BF16),
            pltpu.VMEM((n_y, 2, 2 * depth, half), BF16),
            pltpu.VMEM((2, 2 * n_e * slots, half), F32),
            pltpu.VMEM((2, 2 * n_e * slots, half), BF16),
            pltpu.VMEM((n_dp, count, 8, B), F32),
            pltpu.VMEM((2, n_y // 2, count, 8, B), F32),
            dma(5), dma(2), dma(2), dma(n_e), dma(n_e), dma(groups), dma(groups), dma(2, 2, 2), dma(2, 2, 2),
            dma(2, steps - 1, 2), dma(2, steps - 1, 2), dma(1), dma(1),
            *[dma(2, steps, PIECES)] * 4, *[dma(n_y, PIECES)] * 2,
        ],
        compiler_params=pltpu.CompilerParams(
            collective_id=0, has_side_effects=True, vmem_limit_bytes=48 << 20
        ),
    )(*[pltpu.with_memory_space_constraint(x, pltpu.HBM) for x in (tokens, expert_ids, gate, up)])


def body(tokens, expert_ids, gate_weight, up_weight, down_weight):
    gram = exchange_call(tokens, expert_ids.T, gate_weight[0], up_weight[0])
    place = lax.axis_index("dp").astype(jnp.int32).reshape(1)
    own_rows, whitened = local_call(place, gram, down_weight[0], N // lax.axis_size("dp"))
    return (own_rows[None], whitened[None])


def solution(mesh):
    return jax.shard_map(
        body,
        mesh=mesh,
        in_specs=(
            P(("dp", "expert"), None),
            P(("dp", "expert"), None),
            P("expert", "dp", None),
            P("expert", "dp", None),
            P("expert", None, "dp"),
        ),
        out_specs=(P("expert", "dp", None), P("expert", None, "dp")),
        check_vma=False,
    )
```

```python
import jax
import jax.numpy as jnp
from jax import lax
from jax.experimental import pallas as pl
from jax.experimental.pallas import tpu as pltpu
from jax.sharding import PartitionSpec as P

F32, BF16 = jnp.float32, jnp.bfloat16
N, B, H = 768, 128, 64
CAP = 8
SLOTS = 256
damping = 0.02


def split(x):
    high = x.astype(BF16)
    return high, (x - high.astype(F32)).astype(BF16)


def dot3(left, right, dims):
    lh, ll = split(left)
    rh, rl = split(right)
    left3 = jnp.concatenate([lh, lh, ll], axis=dims[0][0])
    right3 = jnp.concatenate([rh, rl, rh], axis=dims[1][0])
    return lax.dot_general(left3, right3, (dims, ((), ())), preferred_element_type=F32)


NN, TN = ((1,), (0,)), ((0,), (0,))


def eliminate(rows8, first):
    tiles = list(rows8)
    sublane = lax.broadcasted_iota(jnp.int32, (8, 128), 0)
    lane_copy = lambda x, c: jnp.broadcast_to(x[:, c:c + 1], (8, 128))
    row_copy = lambda x, i: jnp.broadcast_to(x[i:i + 1, :], (8, 128))
    columns = [lane_copy(tiles[0], first + j) for j in range(8)]
    for s in range(8):
        base = first + 8 * s
        ahead = [lane_copy(tiles[s + 1], base + 8 + j) for j in range(8)] if s < 7 else []
        a = {(i, j): row_copy(columns[j], i) for j in range(8) for i in range(j, 8)}
        row = [row_copy(tiles[s], j) for j in range(8)]
        inv, low = [], {}
        for j in range(8):
            r = lax.rsqrt(a[j, j])
            inv.append(r)
            for i in range(j + 1, 8):
                low[i, j] = a[i, j] * r
            for jj in range(j + 1, 8):
                for i in range(jj, 8):
                    a[i, jj] = a[i, jj] - low[i, j] * low[jj, j]
            row[j] = row[j] * r
            for i in range(j + 1, 8):
                row[i] = row[i] - low[i, j] * row[j]
        for t in range(s + 1, 8):
            column = [lane_copy(tiles[t], base + j) for j in range(8)]
            total = tiles[t]
            for j in range(8):
                column[j] = column[j] * inv[j]
                for jj in range(j + 1, 8):
                    column[jj] = column[jj] - column[j] * low[jj, j]
                total = total - column[j] * row[j]
                if t == s + 1:
                    ahead = [ahead[k] - column[j] * row_copy(column[j], k) for k in range(8)]
            tiles[t] = total
        columns = ahead
        done = row[0]
        for j in range(1, 8):
            done = jnp.where(sublane == j, row[j], done)
        tiles[s] = done
    return jnp.concatenate(tiles, axis=0)


def factor_block(block):
    lane = lax.broadcasted_iota(jnp.int32, (H, B), 1)
    row = lax.broadcasted_iota(jnp.int32, (H, B), 0)
    zero = jnp.zeros((H, B), F32)
    top, bottom = block[:H], block[H:]
    work = jnp.where(lane < H, top, jnp.where(lane == row + H, 1.0, 0.0))
    done0 = eliminate([work[8 * t:8 * t + 8] for t in range(8)], 0)
    inv0 = jnp.where(lane < H, 0.0, done0)
    upper0 = dot3(inv0, jnp.concatenate([zero, top], axis=0), NN)
    upper0 = jnp.where(lane < H, jnp.where(lane >= row, done0, 0.0), upper0)
    bottom = bottom - dot3(upper0, upper0, TN)[H:]
    mixed = dot3(upper0, inv0, TN)[H:]
    work = jnp.where(lane >= H, bottom, jnp.where(lane == row, 1.0, 0.0))
    done1 = eliminate([work[8 * t:8 * t + 8] for t in range(8)], H)
    upper1 = jnp.where(lane >= row + H, done1, 0.0)
    inv1 = jnp.where(lane < H, done1, 0.0)
    inv1 = inv1 - dot3(inv1, jnp.concatenate([mixed, zero], axis=0), NN)
    return jnp.concatenate([upper0, upper1], axis=0), jnp.concatenate([inv0, inv1], axis=0)


def factor_all(work_ref, down_ref, white_ref):
    count = N // B

    for q in range(count):
        here = slice(q * B, q * B + B)
        upper, inverse = factor_block(work_ref[here, here])
        work_ref[here, here] = upper
        own, after = slice(q * B, q * B + B), slice(q * B + B, N)
        halves = [[part] for part in split(upper)]
        if q < count - 1:
            strip = work_ref[own, after]
            strip = jnp.concatenate([strip[H:], strip[:H]], axis=0)
            strip = dot3(inverse, strip, NN)
            work_ref[own, after] = strip
            high, low = split(strip)
            left3 = jnp.concatenate([high, high, low], axis=0)
            right3 = jnp.concatenate([high, low, high], axis=0)
            for i in range(q + 1, count):
                at = (i - q - 1) * B
                work_ref[i * B:i * B + B, i * B:] -= lax.dot_general(
                    left3[:, at:at + B], right3[:, at:], (TN, ((), ())), preferred_element_type=F32
                )
            halves[0].append(high)
            halves[1].append(low)
        down = down_ref[q * B:, :]
        white_ref[own, :] = jnp.dot(
            jnp.concatenate(halves[0] + halves[1], axis=1), jnp.concatenate([down, down], axis=0),
            preferred_element_type=F32,
        )


def local_kernel(place_ref, gram_ref, down_ref, rows_ref, white_ref, work_ref):
    diagonal = lax.broadcasted_iota(jnp.int32, (B, B), 0) == lax.broadcasted_iota(jnp.int32, (B, B), 1)
    for i in range(N // B):
        for j in range(i, N // B):
            block = gram_ref[:, block_at(i, j)].reshape(B, B) * (1.0 / SLOTS)
            if i == j:
                block = block + jnp.where(diagonal, damping, 0.0)
            work_ref[i * B:i * B + B, j * B:j * B + B] = block
        if i:
            work_ref[i * B:i * B + B, :i * B] = jnp.zeros((B, i * B), F32)
    factor_all(work_ref, down_ref, white_ref)
    share = rows_ref.shape[0]
    rows_ref[...] = work_ref[pl.ds(pl.multiple_of(place_ref[0] * share, 8), share), :]


def local_call(place, gram, down, share=48):
    vmem = pl.BlockSpec(memory_space=pltpu.VMEM)
    return pl.pallas_call(
        local_kernel,
        out_shape=(jax.ShapeDtypeStruct((share, N), F32), jax.ShapeDtypeStruct((N, down.shape[1]), F32)),
        in_specs=[pl.BlockSpec(memory_space=pltpu.SMEM), vmem, vmem],
        out_specs=(vmem, vmem),
        scratch_shapes=[pltpu.VMEM((N, N), F32)],
        compiler_params=pltpu.CompilerParams(vmem_limit_bytes=48 << 20),
    )(place, gram, down)


MESH = pl.DeviceIdType.MESH
PIECES = 2


def block_at(i, j):
    return i * (N // B) - i * (i - 1) // 2 + j - i


def exchange_kernel(
    tokens_ref, ids_ref, gate_ref, up_ref, gram_ref, outgoing_ref, tokens, named, tok, rows, weights, sums, hid, strips, parts,
    own_sem, swap_send, swap_recv, tok_send, tok_recv, pass_send, pass_recv, first_send, first_recv, ring_send, ring_recv,
    hid_send, hid_recv, part_send, part_recv, share_send, share_recv, hand_send, hand_recv,
):
    dp, e = lax.axis_index("dp"), lax.axis_index("expert")
    n_y, n_e = lax.axis_size("dp") // 2, lax.axis_size("expert")
    y, c = lax.div(dp, 2), lax.rem(dp, 2)
    other = 1 - c
    partner = (2 * y + other, e)
    chip = lambda d: lax.rem(y + d + n_y, n_y)
    line = lambda d: (2 * chip(d) + c, e)
    plane = lambda d: (dp, lax.rem(e + d, n_e))

    def remote(src, dst, send, recv, device):
        return pltpu.make_async_remote_copy(src, dst, send, recv, device_id=device, device_id_type=MESH)

    token_load = pltpu.make_async_copy(tokens_ref, tokens, own_sem.at[3])
    token_load.start()
    name_load = pltpu.make_async_copy(ids_ref, named, own_sem.at[4])
    name_load.start()
    barrier = pltpu.get_barrier_semaphore()

    def greet(device):
        pl.semaphore_signal(barrier, inc=1, device_id=device, device_id_type=MESH)

    greet(partner)
    lax.fori_loop(1, n_y, lambda d, _: (greet(line(d)), 0)[1], 0)
    for way in (1, -1):
        greet((2 * chip(way) + other, e))
    lax.fori_loop(1, n_e, lambda d, _: (greet(plane(d)), 0)[1], 0)
    pl.semaphore_wait(barrier, n_y + n_e + 1)

    depth, half = gate_ref.shape[0], gate_ref.shape[1] // 2
    steps = n_y // 2
    mine = pl.ds(pl.multiple_of(c * half, 128), half)
    theirs = pl.ds(pl.multiple_of(other * half, 128), half)
    at = pl.ds(pl.multiple_of(c * depth, depth), depth)
    sources = (gate_ref, up_ref)

    def first(way, g, same):
        k = (1 - way) // 2
        return remote(
            sources[g].at[:, mine if same else theirs], weights.at[y, g, at],
            first_send.at[k, g, 0 if same else 1], first_recv.at[k, g, c],
            (2 * chip(way) + (c if same else other), e),
        )

    def first_in(way, g, source):
        k = (1 - way) // 2
        part = pl.ds(source * depth, depth)
        return remote(
            sources[g].at[:, mine], weights.at[chip(-way), g, part],
            first_send.at[k, g, 0], first_recv.at[k, g, source], line(way),
        )

    for g in range(2):
        for way in (1, -1):
            for same in (True, False):
                first(way, g, same).start()
    swaps = [
        remote(ref.at[:, theirs], weights.at[y, g, at], swap_send.at[g], swap_recv.at[g], partner)
        for g, ref in enumerate(sources)
    ]
    owns = [
        pltpu.make_async_copy(ref.at[:, mine], weights.at[y, g, at], own_sem.at[g])
        for g, ref in enumerate(sources)
    ]
    for copy in swaps + owns:
        copy.start()

    token_load.wait()
    name_load.wait()
    rows_here = tokens.shape[0]
    ids = named[...]
    expert = lax.broadcasted_iota(jnp.int32, (n_e, rows_here), 0)
    member = jnp.zeros((n_e, rows_here), F32)
    for k in range(ids.shape[0]):
        member = member + jnp.where(ids[k:k + 1] == expert, 1.0, 0.0)
    before = lax.broadcasted_iota(jnp.int32, (rows_here, rows_here), 0)
    after = lax.broadcasted_iota(jnp.int32, (rows_here, rows_here), 1)
    earlier = jnp.where(before < after, 1.0, 0.0).astype(BF16)
    rank = jnp.dot(member.astype(BF16), earlier, preferred_element_type=F32)
    place = jnp.where(member > 0.5, rank, -1.0)
    slot = lax.broadcasted_iota(jnp.int32, (CAP, rows_here), 0).astype(F32)
    placing = jnp.concatenate([jnp.where(place[i:i + 1] == slot, 1.0, 0.0) for i in range(n_e)], axis=0).astype(BF16)
    step_width = 512
    for start in range(0, tokens.shape[1], step_width):
        picked = jnp.dot(placing, tokens[:, start:start + step_width], preferred_element_type=F32)
        for i in range(n_e):
            outgoing_ref[i, :, start:start + step_width] = picked[i * CAP:(i + 1) * CAP].astype(BF16)

    def token_copy(d):
        return remote(
            outgoing_ref.at[lax.rem(e + d, n_e)], tok.at[c, e], tok_send.at[d], tok_recv.at[e], plane(d)
        )

    own_tokens = pltpu.make_async_copy(outgoing_ref.at[e], tok.at[c, e], own_sem.at[2])
    own_tokens.start()
    lax.fori_loop(1, n_e, lambda d, _: (token_copy(d).start(), 0)[1], 0)

    def ring(way, step, g, origin):
        k = (1 - way) // 2
        b = chip(-way * (step - 1 + origin))
        return remote(
            weights.at[b, g], weights.at[b, g], ring_send.at[k, step - 2, g], ring_recv.at[k, step - 2, g], line(way)
        )

    def lanes(step):
        return [(1, 0), (-1, 1)] if step == steps else [(1, 0), (-1, 0), (1, 1), (-1, 1)]

    def arrive(step):
        for way, g in lanes(step):
            if step == 1:
                for source in range(2):
                    first_in(way, g, source).wait_recv()
            else:
                ring(way, step, g, 1).wait_recv()
            if step < steps and (way, g) in lanes(step + 1):
                ring(way, step + 1, g, 0).start()

    def multiply(b, g, first=False):
        columns = pl.ds(pl.multiple_of(b * 2 * depth, 2 * depth), 2 * depth)
        product = jnp.dot(rows[:, columns], weights[b, g], preferred_element_type=F32)
        if first:
            sums[g] = product
        else:
            sums[g] += product

    group = n_e // pass_send.shape[0]

    def token_pass(k):
        span = pl.ds(k * group, group)
        return remote(tok.at[c, span], tok.at[c, span], pass_send.at[k], pass_recv.at[k], partner)

    def token_in(k):
        span = pl.ds(k * group, group)
        return remote(tok.at[other, span], tok.at[other, span], pass_send.at[k], pass_recv.at[k], partner)

    def wait_token(source, carry):
        @pl.when(source == e)
        def _():
            own_tokens.wait()

        @pl.when(source != e)
        def _():
            remote(
                outgoing_ref.at[e], tok.at[c, source], tok_send.at[0], tok_recv.at[source], plane(0)
            ).wait_recv()

        return carry

    def settle(k, p):
        pair = jnp.concatenate([tok[k, 2 * p].astype(F32), tok[k, 2 * p + 1].astype(F32)], axis=0)
        rows[pl.ds(pl.multiple_of(k * n_e * 8 + p * 16, 16), 16), :] = pair.astype(BF16)

    arrived_before = max(1, steps - 2)
    for step in range(1, arrived_before + 1):
        arrive(step)
    for k in range(pass_send.shape[0]):
        lax.fori_loop(k * group, (k + 1) * group, wait_token, 0)
        token_pass(k).start()
    lax.fori_loop(0, n_e // 2, lambda p, _: (settle(c, p), 0)[1], 0)
    if arrived_before + 1 < steps:
        arrive(arrived_before + 1)
    for k in range(pass_send.shape[0]):
        token_in(k).wait_recv()
    lax.fori_loop(0, n_e // 2, lambda p, _: (settle(other, p), 0)[1], 0)
    for g in range(2):
        owns[g].wait()
        swaps[g].wait_recv()
        multiply(y, g, True)
    for step in range(1, steps):
        if step > arrived_before + 1:
            arrive(step)
        for way in (1, -1):
            for g in range(2):
                multiply(chip(-way * step), g)
    if steps > arrived_before:
        arrive(steps)
    for g in range(2):
        multiply(chip(steps), g)

    gate_sum, up_sum = sums[0], sums[1]
    hid[c] = (gate_sum / (1.0 + jnp.exp(-gate_sum)) * up_sum).astype(BF16)
    hid_out = remote(hid.at[c], hid.at[c], hid_send.at[0], hid_recv.at[0], partner)
    hid_out.start()
    remote(hid.at[other], hid.at[other], hid_send.at[0], hid_recv.at[0], partner).wait_recv()

    per_half = half // B
    for i in range(N // B):
        left = hid[i // per_half, :, (i % per_half) * B:(i % per_half + 1) * B]
        for h in range(i // per_half, 2):
            begin = i % per_half if h == i // per_half else 0
            product = lax.dot_general(
                left, hid[h, :, begin * B:], (TN, ((), ())), preferred_element_type=F32
            )
            for j in range(per_half - begin):
                strips[:, block_at(i, h * per_half + begin + j)] = product[:, j * B:(j + 1) * B].reshape(16, 8, B)

    count = strips.shape[1]
    cuts = [count * p // PIECES for p in range(PIECES + 1)]
    pieces = [pl.ds(low, high - low) for low, high in zip(cuts, cuts[1:])]
    longest = [1 - 2 * (p % 2) for p in range(PIECES)]
    flows = [(p, way) for p in range(PIECES) for way in (longest[p], -longest[p])]

    def hops(piece, way):
        return steps if way == longest[piece] else steps - 1

    AHEAD, BESIDE, NEAR, JOINED = range(4)
    spans = {AHEAD: (4, 2), BESIDE: (3, 1), NEAR: (1, 1), JOINED: (2, 2)}

    def part(piece, way, kind):
        k, (reach, jump) = (1 - way) // 2, spans[kind]
        return remote(
            strips.at[2 * chip(way * reach) + c, pieces[piece]], parts.at[k, kind, pieces[piece]],
            part_send.at[k, kind, piece], part_recv.at[k, kind, piece], line(way * jump),
        )

    def kinds(piece, way):
        return [AHEAD, BESIDE] if hops(piece, way) == 4 else [BESIDE]

    for piece, way in flows:
        for kind in kinds(piece, way):
            part(piece, way, kind).start()
    for piece, way in flows:
        part(piece, way, NEAR).start()
    for piece, way in flows:
        k, total = (1 - way) // 2, strips[2 * chip(2 * way) + c, pieces[piece]]
        for kind in kinds(piece, way):
            part(piece, way, kind).wait_recv()
            total = total + parts[k, kind, pieces[piece]]
        strips[2 * chip(2 * way) + c, pieces[piece]] = total
        part(piece, way, JOINED).start()

    FIRST, SECOND, THIRD, FOURTH = range(4)
    routes = {FIRST: (0, 1), SECOND: (0, 2), THIRD: (-2, 1), FOURTH: (-2, 2)}

    def share(piece, way, kind, sending):
        k, (source, jump) = (1 - way) // 2, routes[kind]
        strip = gram_ref.at[2 * chip(way * source if sending else way * (source - jump)) + c, pieces[piece]]
        return remote(
            strip, strip, share_send.at[k, kind, piece], share_recv.at[k, kind, piece], line(way * jump)
        )

    def onward(piece, way):
        return [FOURTH, THIRD] if hops(piece, way) == 4 else [THIRD]

    def hand(piece, d, core):
        strip = gram_ref.at[2 * chip(d) + core, pieces[piece]]
        return remote(strip, strip, hand_send.at[d % n_y, piece], hand_recv.at[d % n_y, piece], partner)

    for piece in range(PIECES):
        total = strips[dp, pieces[piece]]
        for kind in (NEAR, JOINED):
            for way in (1, -1):
                part(piece, way, kind).wait_recv()
                total = total + parts[(1 - way) // 2, kind, pieces[piece]]
        gram_ref[dp, pieces[piece]] = total
        for kind in (SECOND, FIRST):
            for way in (1, -1):
                share(piece, way, kind, True).start()
        hand(piece, 0, c).start()
    for piece, way in flows:
        share(piece, way, SECOND, False).wait_recv()
        for kind in onward(piece, way):
            share(piece, way, kind, True).start()
        hand(piece, -2 * way, c).start()
    for piece, way in flows:
        share(piece, way, FIRST, False).wait_recv()
        hand(piece, -way, c).start()
    for piece, way in flows:
        for kind in onward(piece, way)[::-1]:
            share(piece, way, kind, False).wait_recv()
            hand(piece, -way * (3 if kind == THIRD else 4), c).start()
    for d in range(n_y):
        for piece in range(PIECES):
            hand(piece, d, other).wait_recv()

    for copy in swaps:
        copy.wait_send()
    for g in range(2):
        for way in (1, -1):
            for same in (True, False):
                first(way, g, same).wait_send()
    lax.fori_loop(1, n_e, lambda d, _: (token_copy(d).wait_send(), 0)[1], 0)
    for k in range(pass_send.shape[0]):
        token_pass(k).wait_send()
    for step in range(2, steps + 1):
        for way, g in lanes(step):
            ring(way, step, g, 0).wait_send()
    hid_out.wait_send()
    for piece, way in flows:
        for kind in kinds(piece, way) + [NEAR, JOINED]:
            part(piece, way, kind).wait_send()
        for kind in onward(piece, way) + [FIRST, SECOND]:
            share(piece, way, kind, True).wait_send()
    for d in range(n_y):
        for piece in range(PIECES):
            hand(piece, d, c).wait_send()


def exchange_call(tokens, expert_ids, gate, up):
    n_dp, n_e = lax.axis_size("dp"), lax.axis_size("expert")
    slots, width = CAP, tokens.shape[1]
    n_y, depth, half = n_dp // 2, gate.shape[0], gate.shape[1] // 2
    count = (N // B) * (N // B + 1) // 2
    groups, steps = 4, n_y // 2
    dma = lambda *shape: pltpu.SemaphoreType.DMA(shape)
    vmem, anywhere = pl.BlockSpec(memory_space=pltpu.VMEM), pl.BlockSpec(memory_space=pltpu.HBM)
    return pl.pallas_call(
        exchange_kernel,
        out_shape=jax.ShapeDtypeStruct((n_dp, count, 8, B), F32),
        in_specs=[anywhere] * 4,
        out_specs=vmem,
        scratch_shapes=[
            pltpu.VMEM((n_e, slots, width), BF16),
            pltpu.VMEM(tokens.shape, BF16),
            pltpu.VMEM(expert_ids.shape, jnp.int32),
            pltpu.VMEM((2, n_e, slots, width), BF16),
            pltpu.VMEM((2 * n_e * slots, width), BF16),
            pltpu.VMEM((n_y, 2, 2 * depth, half), BF16),
            pltpu.VMEM((2, 2 * n_e * slots, half), F32),
            pltpu.VMEM((2, 2 * n_e * slots, half), BF16),
            pltpu.VMEM((n_dp, count, 8, B), F32),
            pltpu.VMEM((2, n_y // 2, count, 8, B), F32),
            dma(5), dma(2), dma(2), dma(n_e), dma(n_e), dma(groups), dma(groups), dma(2, 2, 2), dma(2, 2, 2),
            dma(2, steps - 1, 2), dma(2, steps - 1, 2), dma(1), dma(1),
            *[dma(2, steps, PIECES)] * 4, *[dma(n_y, PIECES)] * 2,
        ],
        compiler_params=pltpu.CompilerParams(
            collective_id=0, has_side_effects=True, vmem_limit_bytes=48 << 20
        ),
    )(*[pltpu.with_memory_space_constraint(x, pltpu.HBM) for x in (tokens, expert_ids, gate, up)])


def body(tokens, expert_ids, gate_weight, up_weight, down_weight):
    gram = exchange_call(tokens, expert_ids.T, gate_weight[0], up_weight[0])
    place = lax.axis_index("dp").astype(jnp.int32).reshape(1)
    own_rows, whitened = local_call(place, gram, down_weight[0], N // lax.axis_size("dp"))
    return (own_rows[None], whitened[None])


def solution(mesh):
    return jax.shard_map(
        body,
        mesh=mesh,
        in_specs=(
            P(("dp", "expert"), None),
            P(("dp", "expert"), None),
            P("expert", "dp", None),
            P("expert", "dp", None),
            P("expert", None, "dp"),
        ),
        out_specs=(P("expert", "dp", None), P("expert", None, "dp")),
        check_vma=False,
    )
```

```python
import jax
import jax.numpy as jnp
from jax import lax
from jax.experimental import pallas as pl
from jax.experimental.pallas import tpu as pltpu
from jax.sharding import PartitionSpec as P

F32, BF16 = jnp.float32, jnp.bfloat16
N, B, H = 768, 128, 64
CAP = 8
SLOTS = 256
damping = 0.02


def split(x):
    high = x.astype(BF16)
    return high, (x - high.astype(F32)).astype(BF16)


def dot3(left, right, dims):
    lh, ll = split(left)
    rh, rl = split(right)
    left3 = jnp.concatenate([lh, lh, ll], axis=dims[0][0])
    right3 = jnp.concatenate([rh, rl, rh], axis=dims[1][0])
    return lax.dot_general(left3, right3, (dims, ((), ())), preferred_element_type=F32)


NN, TN = ((1,), (0,)), ((0,), (0,))


def eliminate(rows8, first):
    tiles = list(rows8)
    sublane = lax.broadcasted_iota(jnp.int32, (8, 128), 0)
    lane_copy = lambda x, c: jnp.broadcast_to(x[:, c:c + 1], (8, 128))
    row_copy = lambda x, i: jnp.broadcast_to(x[i:i + 1, :], (8, 128))
    columns = [lane_copy(tiles[0], first + j) for j in range(8)]
    for s in range(8):
        base = first + 8 * s
        ahead = [lane_copy(tiles[s + 1], base + 8 + j) for j in range(8)] if s < 7 else []
        a = {(i, j): row_copy(columns[j], i) for j in range(8) for i in range(j, 8)}
        row = [row_copy(tiles[s], j) for j in range(8)]
        inv, low = [], {}
        for j in range(8):
            r = lax.rsqrt(a[j, j])
            inv.append(r)
            for i in range(j + 1, 8):
                low[i, j] = a[i, j] * r
            for jj in range(j + 1, 8):
                for i in range(jj, 8):
                    a[i, jj] = a[i, jj] - low[i, j] * low[jj, j]
            row[j] = row[j] * r
            for i in range(j + 1, 8):
                row[i] = row[i] - low[i, j] * row[j]
        for t in range(s + 1, 8):
            column = [lane_copy(tiles[t], base + j) for j in range(8)]
            total = tiles[t]
            for j in range(8):
                column[j] = column[j] * inv[j]
                for jj in range(j + 1, 8):
                    column[jj] = column[jj] - column[j] * low[jj, j]
                total = total - column[j] * row[j]
                if t == s + 1:
                    ahead = [ahead[k] - column[j] * row_copy(column[j], k) for k in range(8)]
            tiles[t] = total
        columns = ahead
        done = row[0]
        for j in range(1, 8):
            done = jnp.where(sublane == j, row[j], done)
        tiles[s] = done
    return jnp.concatenate(tiles, axis=0)


def factor_block(block):
    lane = lax.broadcasted_iota(jnp.int32, (H, B), 1)
    row = lax.broadcasted_iota(jnp.int32, (H, B), 0)
    zero = jnp.zeros((H, B), F32)
    top, bottom = block[:H], block[H:]
    work = jnp.where(lane < H, top, jnp.where(lane == row + H, 1.0, 0.0))
    done0 = eliminate([work[8 * t:8 * t + 8] for t in range(8)], 0)
    inv0 = jnp.where(lane < H, 0.0, done0)
    upper0 = dot3(inv0, jnp.concatenate([zero, top], axis=0), NN)
    upper0 = jnp.where(lane < H, jnp.where(lane >= row, done0, 0.0), upper0)
    bottom = bottom - dot3(upper0, upper0, TN)[H:]
    mixed = dot3(upper0, inv0, TN)[H:]
    work = jnp.where(lane >= H, bottom, jnp.where(lane == row, 1.0, 0.0))
    done1 = eliminate([work[8 * t:8 * t + 8] for t in range(8)], H)
    upper1 = jnp.where(lane >= row + H, done1, 0.0)
    inv1 = jnp.where(lane < H, done1, 0.0)
    inv1 = inv1 - dot3(inv1, jnp.concatenate([mixed, zero], axis=0), NN)
    return jnp.concatenate([upper0, upper1], axis=0), jnp.concatenate([inv0, inv1], axis=0)


def factor_all(work_ref, down_ref, white_ref):
    count = N // B

    for q in range(count):
        here = slice(q * B, q * B + B)
        upper, inverse = factor_block(work_ref[here, here])
        work_ref[here, here] = upper
        own, after = slice(q * B, q * B + B), slice(q * B + B, N)
        halves = [[part] for part in split(upper)]
        if q < count - 1:
            strip = work_ref[own, after]
            strip = jnp.concatenate([strip[H:], strip[:H]], axis=0)
            strip = dot3(inverse, strip, NN)
            work_ref[own, after] = strip
            high, low = split(strip)
            left3 = jnp.concatenate([high, high, low], axis=0)
            right3 = jnp.concatenate([high, low, high], axis=0)
            for i in range(q + 1, count):
                at = (i - q - 1) * B
                work_ref[i * B:i * B + B, i * B:] -= lax.dot_general(
                    left3[:, at:at + B], right3[:, at:], (TN, ((), ())), preferred_element_type=F32
                )
            halves[0].append(high)
            halves[1].append(low)
        down = down_ref[q * B:, :]
        white_ref[own, :] = jnp.dot(
            jnp.concatenate(halves[0] + halves[1], axis=1), jnp.concatenate([down, down], axis=0),
            preferred_element_type=F32,
        )


def local_kernel(place_ref, gram_ref, down_ref, rows_ref, white_ref, work_ref):
    diagonal = lax.broadcasted_iota(jnp.int32, (B, B), 0) == lax.broadcasted_iota(jnp.int32, (B, B), 1)
    for i in range(N // B):
        for j in range(i, N // B):
            block = gram_ref[:, block_at(i, j)].reshape(B, B) * (1.0 / SLOTS)
            if i == j:
                block = block + jnp.where(diagonal, damping, 0.0)
            work_ref[i * B:i * B + B, j * B:j * B + B] = block
        if i:
            work_ref[i * B:i * B + B, :i * B] = jnp.zeros((B, i * B), F32)
    factor_all(work_ref, down_ref, white_ref)
    share = rows_ref.shape[0]
    rows_ref[...] = work_ref[pl.ds(pl.multiple_of(place_ref[0] * share, 8), share), :]


def local_call(place, gram, down, share=48):
    vmem = pl.BlockSpec(memory_space=pltpu.VMEM)
    return pl.pallas_call(
        local_kernel,
        out_shape=(jax.ShapeDtypeStruct((share, N), F32), jax.ShapeDtypeStruct((N, down.shape[1]), F32)),
        in_specs=[pl.BlockSpec(memory_space=pltpu.SMEM), vmem, vmem],
        out_specs=(vmem, vmem),
        scratch_shapes=[pltpu.VMEM((N, N), F32)],
        compiler_params=pltpu.CompilerParams(vmem_limit_bytes=48 << 20),
    )(place, gram, down)


MESH = pl.DeviceIdType.MESH
PIECES = 2


def block_at(i, j):
    return i * (N // B) - i * (i - 1) // 2 + j - i


def exchange_kernel(
    tokens_ref, ids_ref, gate_ref, up_ref, gram_ref, outgoing_ref, tokens, named, tok, rows, weights, sums, hid, strips, parts,
    own_sem, swap_send, swap_recv, tok_send, tok_recv, pass_send, pass_recv, first_send, first_recv, ring_send, ring_recv,
    hid_send, hid_recv, part_send, part_recv, share_send, share_recv, hand_send, hand_recv,
):
    dp, e = lax.axis_index("dp"), lax.axis_index("expert")
    n_y, n_e = lax.axis_size("dp") // 2, lax.axis_size("expert")
    y, c = lax.div(dp, 2), lax.rem(dp, 2)
    other = 1 - c
    partner = (2 * y + other, e)
    chip = lambda d: lax.rem(y + d + n_y, n_y)
    line = lambda d: (2 * chip(d) + c, e)
    plane = lambda d: (dp, lax.rem(e + d, n_e))

    def remote(src, dst, send, recv, device):
        return pltpu.make_async_remote_copy(src, dst, send, recv, device_id=device, device_id_type=MESH)

    token_load = pltpu.make_async_copy(tokens_ref, tokens, own_sem.at[3])
    token_load.start()
    name_load = pltpu.make_async_copy(ids_ref, named, own_sem.at[4])
    name_load.start()
    barrier = pltpu.get_barrier_semaphore()

    def greet(device):
        pl.semaphore_signal(barrier, inc=1, device_id=device, device_id_type=MESH)

    greet(partner)
    lax.fori_loop(1, n_y, lambda d, _: (greet(line(d)), 0)[1], 0)
    for way in (1, -1):
        greet((2 * chip(way) + other, e))
    lax.fori_loop(1, n_e, lambda d, _: (greet(plane(d)), 0)[1], 0)
    pl.semaphore_wait(barrier, n_y + n_e + 1)

    depth, half = gate_ref.shape[0], gate_ref.shape[1] // 2
    steps = n_y // 2
    mine = pl.ds(pl.multiple_of(c * half, 128), half)
    theirs = pl.ds(pl.multiple_of(other * half, 128), half)
    at = pl.ds(pl.multiple_of(c * depth, depth), depth)
    sources = (gate_ref, up_ref)

    def first(way, g, same):
        k = (1 - way) // 2
        return remote(
            sources[g].at[:, mine if same else theirs], weights.at[y, g, at],
            first_send.at[k, g, 0 if same else 1], first_recv.at[k, g, c],
            (2 * chip(way) + (c if same else other), e),
        )

    def first_in(way, g, source):
        k = (1 - way) // 2
        part = pl.ds(source * depth, depth)
        return remote(
            sources[g].at[:, mine], weights.at[chip(-way), g, part],
            first_send.at[k, g, 0], first_recv.at[k, g, source], line(way),
        )

    for g in range(2):
        for way in (1, -1):
            for same in (True, False):
                first(way, g, same).start()
    swaps = [
        remote(ref.at[:, theirs], weights.at[y, g, at], swap_send.at[g], swap_recv.at[g], partner)
        for g, ref in enumerate(sources)
    ]
    owns = [
        pltpu.make_async_copy(ref.at[:, mine], weights.at[y, g, at], own_sem.at[g])
        for g, ref in enumerate(sources)
    ]
    for copy in swaps + owns:
        copy.start()

    token_load.wait()
    name_load.wait()
    rows_here = tokens.shape[0]
    ids = named[...]
    expert = lax.broadcasted_iota(jnp.int32, (n_e, rows_here), 0)
    member = jnp.zeros((n_e, rows_here), F32)
    for k in range(ids.shape[0]):
        member = member + jnp.where(ids[k:k + 1] == expert, 1.0, 0.0)
    before = lax.broadcasted_iota(jnp.int32, (rows_here, rows_here), 0)
    after = lax.broadcasted_iota(jnp.int32, (rows_here, rows_here), 1)
    earlier = jnp.where(before < after, 1.0, 0.0).astype(BF16)
    rank = jnp.dot(member.astype(BF16), earlier, preferred_element_type=F32)
    place = jnp.where(member > 0.5, rank, -1.0)
    slot = lax.broadcasted_iota(jnp.int32, (CAP, rows_here), 0).astype(F32)
    placing = jnp.concatenate([jnp.where(place[i:i + 1] == slot, 1.0, 0.0) for i in range(n_e)], axis=0).astype(BF16)
    step_width = 512
    for start in range(0, tokens.shape[1], step_width):
        picked = jnp.dot(placing, tokens[:, start:start + step_width], preferred_element_type=F32)
        for i in range(n_e):
            outgoing_ref[i, :, start:start + step_width] = picked[i * CAP:(i + 1) * CAP].astype(BF16)

    def token_copy(d):
        return remote(
            outgoing_ref.at[lax.rem(e + d, n_e)], tok.at[c, e], tok_send.at[d], tok_recv.at[e], plane(d)
        )

    own_tokens = pltpu.make_async_copy(outgoing_ref.at[e], tok.at[c, e], own_sem.at[2])
    own_tokens.start()
    lax.fori_loop(1, n_e, lambda d, _: (token_copy(d).start(), 0)[1], 0)

    def ring(way, step, g, origin):
        k = (1 - way) // 2
        b = chip(-way * (step - 1 + origin))
        return remote(
            weights.at[b, g], weights.at[b, g], ring_send.at[k, step - 2, g], ring_recv.at[k, step - 2, g], line(way)
        )

    def lanes(step):
        return [(1, 0), (-1, 1)] if step == steps else [(1, 0), (-1, 0), (1, 1), (-1, 1)]

    def arrive(step):
        for way, g in lanes(step):
            if step == 1:
                for source in range(2):
                    first_in(way, g, source).wait_recv()
            else:
                ring(way, step, g, 1).wait_recv()
            if step < steps and (way, g) in lanes(step + 1):
                ring(way, step + 1, g, 0).start()

    def multiply(b, g, first=False):
        columns = pl.ds(pl.multiple_of(b * 2 * depth, 2 * depth), 2 * depth)
        product = jnp.dot(rows[:, columns], weights[b, g], preferred_element_type=F32)
        if first:
            sums[g] = product
        else:
            sums[g] += product

    group = n_e // pass_send.shape[0]

    def token_pass(k):
        span = pl.ds(k * group, group)
        return remote(tok.at[c, span], tok.at[c, span], pass_send.at[k], pass_recv.at[k], partner)

    def token_in(k):
        span = pl.ds(k * group, group)
        return remote(tok.at[other, span], tok.at[other, span], pass_send.at[k], pass_recv.at[k], partner)

    def wait_token(source, carry):
        @pl.when(source == e)
        def _():
            own_tokens.wait()

        @pl.when(source != e)
        def _():
            remote(
                outgoing_ref.at[e], tok.at[c, source], tok_send.at[0], tok_recv.at[source], plane(0)
            ).wait_recv()

        return carry

    def settle(k, p):
        pair = jnp.concatenate([tok[k, 2 * p].astype(F32), tok[k, 2 * p + 1].astype(F32)], axis=0)
        rows[pl.ds(pl.multiple_of(k * n_e * 8 + p * 16, 16), 16), :] = pair.astype(BF16)

    arrived_before = max(1, steps - 2)
    for step in range(1, arrived_before + 1):
        arrive(step)
    for k in range(pass_send.shape[0]):
        lax.fori_loop(k * group, (k + 1) * group, wait_token, 0)
        token_pass(k).start()
    lax.fori_loop(0, n_e // 2, lambda p, _: (settle(c, p), 0)[1], 0)
    if arrived_before + 1 < steps:
        arrive(arrived_before + 1)
    for k in range(pass_send.shape[0]):
        token_in(k).wait_recv()
    lax.fori_loop(0, n_e // 2, lambda p, _: (settle(other, p), 0)[1], 0)
    for g in range(2):
        owns[g].wait()
        swaps[g].wait_recv()
        multiply(y, g, True)
    for step in range(1, steps):
        if step > arrived_before + 1:
            arrive(step)
        for way in (1, -1):
            for g in range(2):
                multiply(chip(-way * step), g)
    if steps > arrived_before:
        arrive(steps)
    for g in range(2):
        multiply(chip(steps), g)

    tall = rows.shape[0] // 2

    def hid_copy(k, core):
        span = hid.at[core, pl.ds(k * tall, tall)]
        return remote(span, span, hid_send.at[k], hid_recv.at[k], partner)

    for k in range(2):
        span = slice(k * tall, k * tall + tall)
        gate_sum, up_sum = sums[0, span], sums[1, span]
        hid[c, span] = (gate_sum / (1.0 + jnp.exp(-gate_sum)) * up_sum).astype(BF16)
        hid_copy(k, c).start()
    for k in range(2):
        hid_copy(k, other).wait_recv()

    per_half = half // B
    for i in range(N // B):
        left = hid[i // per_half, :, (i % per_half) * B:(i % per_half + 1) * B]
        for h in range(i // per_half, 2):
            begin = i % per_half if h == i // per_half else 0
            product = lax.dot_general(
                left, hid[h, :, begin * B:], (TN, ((), ())), preferred_element_type=F32
            )
            for j in range(per_half - begin):
                strips[:, block_at(i, h * per_half + begin + j)] = product[:, j * B:(j + 1) * B].reshape(16, 8, B)

    count = strips.shape[1]
    cuts = [count * p // PIECES for p in range(PIECES + 1)]
    pieces = [pl.ds(low, high - low) for low, high in zip(cuts, cuts[1:])]
    longest = [1 - 2 * (p % 2) for p in range(PIECES)]
    flows = [(p, way) for p in range(PIECES) for way in (longest[p], -longest[p])]

    def hops(piece, way):
        return steps if way == longest[piece] else steps - 1

    AHEAD, BESIDE, NEAR, JOINED = range(4)
    spans = {AHEAD: (4, 2), BESIDE: (3, 1), NEAR: (1, 1), JOINED: (2, 2)}

    def part(piece, way, kind):
        k, (reach, jump) = (1 - way) // 2, spans[kind]
        return remote(
            strips.at[2 * chip(way * reach) + c, pieces[piece]], parts.at[k, kind, pieces[piece]],
            part_send.at[k, kind, piece], part_recv.at[k, kind, piece], line(way * jump),
        )

    def kinds(piece, way):
        return [AHEAD, BESIDE] if hops(piece, way) == 4 else [BESIDE]

    for piece, way in flows:
        for kind in kinds(piece, way):
            part(piece, way, kind).start()
    for piece, way in flows:
        part(piece, way, NEAR).start()
    for piece, way in flows:
        k, total = (1 - way) // 2, strips[2 * chip(2 * way) + c, pieces[piece]]
        for kind in kinds(piece, way):
            part(piece, way, kind).wait_recv()
            total = total + parts[k, kind, pieces[piece]]
        strips[2 * chip(2 * way) + c, pieces[piece]] = total
        part(piece, way, JOINED).start()

    FIRST, SECOND, THIRD, FOURTH = range(4)
    routes = {FIRST: (0, 1), SECOND: (0, 2), THIRD: (-2, 1), FOURTH: (-2, 2)}

    def share(piece, way, kind, sending):
        k, (source, jump) = (1 - way) // 2, routes[kind]
        strip = gram_ref.at[2 * chip(way * source if sending else way * (source - jump)) + c, pieces[piece]]
        return remote(
            strip, strip, share_send.at[k, kind, piece], share_recv.at[k, kind, piece], line(way * jump)
        )

    def onward(piece, way):
        return [FOURTH, THIRD] if hops(piece, way) == 4 else [THIRD]

    def hand(piece, d, core):
        strip = gram_ref.at[2 * chip(d) + core, pieces[piece]]
        return remote(strip, strip, hand_send.at[d % n_y, piece], hand_recv.at[d % n_y, piece], partner)

    for piece in range(PIECES):
        total = strips[dp, pieces[piece]]
        for kind in (NEAR, JOINED):
            for way in (1, -1):
                part(piece, way, kind).wait_recv()
                total = total + parts[(1 - way) // 2, kind, pieces[piece]]
        gram_ref[dp, pieces[piece]] = total
        for kind in (SECOND, FIRST):
            for way in (1, -1):
                share(piece, way, kind, True).start()
        hand(piece, 0, c).start()
    for piece, way in flows:
        share(piece, way, SECOND, False).wait_recv()
        for kind in onward(piece, way):
            share(piece, way, kind, True).start()
        hand(piece, -2 * way, c).start()
    for piece, way in flows:
        share(piece, way, FIRST, False).wait_recv()
        hand(piece, -way, c).start()
    for piece, way in flows:
        for kind in onward(piece, way)[::-1]:
            share(piece, way, kind, False).wait_recv()
            hand(piece, -way * (3 if kind == THIRD else 4), c).start()
    for d in range(n_y):
        for piece in range(PIECES):
            hand(piece, d, other).wait_recv()

    for copy in swaps:
        copy.wait_send()
    for g in range(2):
        for way in (1, -1):
            for same in (True, False):
                first(way, g, same).wait_send()
    lax.fori_loop(1, n_e, lambda d, _: (token_copy(d).wait_send(), 0)[1], 0)
    for k in range(pass_send.shape[0]):
        token_pass(k).wait_send()
    for step in range(2, steps + 1):
        for way, g in lanes(step):
            ring(way, step, g, 0).wait_send()
    for k in range(2):
        hid_copy(k, c).wait_send()
    for piece, way in flows:
        for kind in kinds(piece, way) + [NEAR, JOINED]:
            part(piece, way, kind).wait_send()
        for kind in onward(piece, way) + [FIRST, SECOND]:
            share(piece, way, kind, True).wait_send()
    for d in range(n_y):
        for piece in range(PIECES):
            hand(piece, d, c).wait_send()


def exchange_call(tokens, expert_ids, gate, up):
    n_dp, n_e = lax.axis_size("dp"), lax.axis_size("expert")
    slots, width = CAP, tokens.shape[1]
    n_y, depth, half = n_dp // 2, gate.shape[0], gate.shape[1] // 2
    count = (N // B) * (N // B + 1) // 2
    groups, steps = 4, n_y // 2
    dma = lambda *shape: pltpu.SemaphoreType.DMA(shape)
    vmem, anywhere = pl.BlockSpec(memory_space=pltpu.VMEM), pl.BlockSpec(memory_space=pltpu.HBM)
    return pl.pallas_call(
        exchange_kernel,
        out_shape=jax.ShapeDtypeStruct((n_dp, count, 8, B), F32),
        in_specs=[anywhere] * 4,
        out_specs=vmem,
        scratch_shapes=[
            pltpu.VMEM((n_e, slots, width), BF16),
            pltpu.VMEM(tokens.shape, BF16),
            pltpu.VMEM(expert_ids.shape, jnp.int32),
            pltpu.VMEM((2, n_e, slots, width), BF16),
            pltpu.VMEM((2 * n_e * slots, width), BF16),
            pltpu.VMEM((n_y, 2, 2 * depth, half), BF16),
            pltpu.VMEM((2, 2 * n_e * slots, half), F32),
            pltpu.VMEM((2, 2 * n_e * slots, half), BF16),
            pltpu.VMEM((n_dp, count, 8, B), F32),
            pltpu.VMEM((2, n_y // 2, count, 8, B), F32),
            dma(5), dma(2), dma(2), dma(n_e), dma(n_e), dma(groups), dma(groups), dma(2, 2, 2), dma(2, 2, 2),
            dma(2, steps - 1, 2), dma(2, steps - 1, 2), dma(2), dma(2),
            *[dma(2, steps, PIECES)] * 4, *[dma(n_y, PIECES)] * 2,
        ],
        compiler_params=pltpu.CompilerParams(
            collective_id=0, has_side_effects=True, vmem_limit_bytes=48 << 20
        ),
    )(*[pltpu.with_memory_space_constraint(x, pltpu.HBM) for x in (tokens, expert_ids, gate, up)])


def body(tokens, expert_ids, gate_weight, up_weight, down_weight):
    gram = exchange_call(tokens, expert_ids.T, gate_weight[0], up_weight[0])
    place = lax.axis_index("dp").astype(jnp.int32).reshape(1)
    own_rows, whitened = local_call(place, gram, down_weight[0], N // lax.axis_size("dp"))
    return (own_rows[None], whitened[None])


def solution(mesh):
    return jax.shard_map(
        body,
        mesh=mesh,
        in_specs=(
            P(("dp", "expert"), None),
            P(("dp", "expert"), None),
            P("expert", "dp", None),
            P("expert", "dp", None),
            P("expert", None, "dp"),
        ),
        out_specs=(P("expert", "dp", None), P("expert", None, "dp")),
        check_vma=False,
    )
```
